32 devices in a mesh: frames: 8 (over y, x, core), chan: 4 (over z).
Axes of the slice: x: 2, y: 2, z: 4, core: 2. Of those that a mesh axis runs over, the one named last changes fastest.
Arguments:
- inputs: bfloat16 [16, 256, 16, 128], P('frames', 'chan'), may hold values from -6 to 6
- saved: bfloat16 [16, 256, 16, 128], P('frames', 'chan'), may hold values from -6 to 6
- cotangent: bfloat16 [8, 256, 512], P('frames', 'chan'), may hold values from -24 to 24
- spatial_w: bfloat16 [3, 3, 256, 256], P(None, None, 'chan'), may hold values from -0.125 to 0.125
- temporal_w: bfloat16 [3, 256, 256], replicated, may hold values from -0.21875 to 0.21875
Outputs:
- input_grad: bfloat16 [16, 256, 16, 128], P('frames', 'chan')
- spatial_grad: float32 [3, 3, 256, 256], P(None, None, 'chan')
- temporal_grad: float32 [3, 256, 256], P(None, 'chan')
The draws below stay inside these ranges and needn't reach their ends.
All inputs are finite; a program needn't handle non-finite values.
Results may differ from the reference program's by a relative error of at most 0.0049.
Values may be sent and summed in bfloat16 or wider, within the bound.
No kernel may reach another device: no remote copies, remote signals or barrier semaphores. Data moves between devices by JAX's collectives and lax.ppermute only.
A program may use at most 64 MiB of HBM per device.

```python
import math
import jax
import jax.numpy as jnp

C = 256
W = 128
H = 16
FRAMES = 16
POOLED = 512


def levels(key, dims, pieces, low, high):
    gain = 1.0
    for position, shards_of in pieces:
        draws = jax.random.uniform(jax.random.fold_in(jax.random.fold_in(key, 6), position), (shards_of,), jnp.float32, low / len(pieces), high / len(pieces))
        gain = gain * jnp.repeat(jnp.exp(draws), dims[position] // shards_of).reshape((-1,) + (1,) * (len(dims) - 1 - position))
    return gain


def noise(rng, shape, width, most, split=(), dtype=jnp.bfloat16):
    values = width * jax.random.normal(rng, shape, jnp.float32)
    if split:
        values = values * levels(rng, shape, split, -0.22, 0.18)
    return jnp.clip(values, -most, most).astype(dtype)


def setup_inputs(seed: int = 0) -> dict:
    key_list = jax.random.split(jax.random.key(seed), 6)
    return {
        "inputs": noise(key_list[0], (FRAMES, C, H, W), 1.0, 6.0, ((0, 8), (1, 4))),
        "saved": noise(key_list[1], (FRAMES, C, H, W), 1.0, 6.0, ((0, 8), (1, 4))),
        "cotangent": noise(key_list[2], (FRAMES // 2, C, POOLED), 4.0, 24.0, ((0, 8), (1, 4))),
        "spatial_w": noise(key_list[3], (3, 3, C, C), (9 * C) ** -0.5, 0.125, ((2, 4),)),
        "temporal_w": noise(key_list[4], (3, C, C), (3 * C) ** -0.5, 0.21875),
    }


def reference(inputs, saved, cotangent, spatial_w, temporal_w):
    wide = jnp.float32
    scale = 1.0 / math.sqrt(FRAMES * H * W)
    half = cotangent.reshape(FRAMES // 2, C, H // 2, W // 2).astype(wide) * 0.125
    upsampled = jnp.repeat(jnp.repeat(jnp.repeat(half, 2, axis=0), 2, axis=2), 2, axis=3).astype(jnp.bfloat16)
    frame_pad = ((1, 1), (0, 0), (0, 0), (0, 0))
    up_pad = jnp.pad(upsampled.astype(wide), frame_pad)
    saved_pad = jnp.pad(saved.astype(wide), frame_pad)
    wide_t = temporal_w.astype(wide)
    grad_sum = jnp.zeros((FRAMES, C, H, W), wide)
    for tap in range(3):
        grad_sum = grad_sum + jnp.einsum('fohw,io->fihw', up_pad[2 - tap:2 - tap + FRAMES], wide_t[tap])
    saved_grad = grad_sum.astype(jnp.bfloat16)
    temporal_grad = jnp.stack([jnp.einsum('fihw,fohw->io', saved_pad[tap:tap + FRAMES], up_pad[1:FRAMES + 1]) for tap in range(3)]) * scale
    space_pad = ((0, 0), (0, 0), (1, 1), (1, 1))
    grad_wide = saved_grad.astype(wide)
    grad_pad = jnp.pad(grad_wide, space_pad)
    input_pad = jnp.pad(inputs.astype(wide), space_pad)
    wide_s = spatial_w.astype(wide)
    input_sum = jnp.zeros((FRAMES, C, H, W), wide)
    kernel_rows = []
    for tap_row in range(3):
        kernel_cols = []
        for tap_col in range(3):
            window = grad_pad[:, :, 2 - tap_row:2 - tap_row + H, 2 - tap_col:2 - tap_col + W]
            input_sum = input_sum + jnp.einsum('fohw,io->fihw', window, wide_s[tap_row, tap_col])
            shifted = input_pad[:, :, tap_row:tap_row + H, tap_col:tap_col + W]
            kernel_cols.append(jnp.einsum('fihw,fohw->io', shifted, grad_wide))
        kernel_rows.append(jnp.stack(kernel_cols))
    spatial_grad = jnp.stack(kernel_rows) * scale
    return (input_sum.astype(jnp.bfloat16), spatial_grad, temporal_grad)
```

```python
import functools
import math

import jax
import jax.numpy as jnp
from jax import lax
from jax.experimental import pallas as pl
from jax.experimental.pallas import tpu as pltpu
from jax.sharding import PartitionSpec as P

F32, BF16 = jnp.float32, jnp.bfloat16
LANES = 128


def one_hot_pool(slots, shifts, cols):
    half = LANES // 2
    shape = (slots * cols, len(shifts) * LANES)
    row = lax.broadcasted_iota(jnp.int32, shape, 0)
    col = lax.broadcasted_iota(jnp.int32, shape, 1)
    slot, w = row // cols, row % cols
    which, lane = col // LANES, col % LANES
    first = 2 * (lane % half) + which + (shifts[0] - 1)
    hit = (slot // 2 == lane // half) & ((w == first) | (w == first + 1))
    return jnp.where(hit, 1.0, 0.0).astype(BF16)


def one_hot_spread(cols):
    half = LANES // 2
    shape = (LANES, 3 * 2 * cols)
    row = lax.broadcasted_iota(jnp.int32, shape, 0)
    col = lax.broadcasted_iota(jnp.int32, shape, 1)
    tap, pair, w = col // (2 * cols), (col // cols) % 2, col % cols
    at = w - tap + 1
    hit = (at >= 0) & (at < cols) & (row == pair * half + at // 2)
    return jnp.where(hit, 1.0, 0.0).astype(BF16)


def prep_kernel(x_ref, y_ref, sw_ref, s_ref, p_ref, wc_ref, rows, left):
    frames, chans, height, cols = x_ref.shape
    steps = height // 4
    zero = jnp.zeros((chans, cols), BF16)
    pool = one_hot_pool(4, (0, 1, 2), cols)

    def place(a, f, h, value):
        t, slot = (h - a + 1) // 4, (h - a + 1) % 4
        if 0 <= t < steps:
            at = (f * steps + t) * chans
            left[a, at : at + chans, slot * cols : (slot + 1) * cols] = value

    rows[...] = y_ref[...].reshape(frames * chans * height, cols).astype(F32)
    for f in range(frames):
        for h in range(height):
            at = f * chans * height + h
            place(1, f, h, rows[pl.ds(at, chans, stride=height), :].astype(BF16))
    done = jnp.dot(left[1], pool[:, LANES : 2 * LANES], preferred_element_type=F32).astype(BF16)
    for f in range(frames):
        for t in range(steps):
            at = (f * steps + t) * chans
            p_ref[f, :, t * LANES : (t + 1) * LANES] = done[at : at + chans]

    rows[...] = x_ref[...].reshape(frames * chans * height, cols).astype(F32)
    for f in range(frames):
        for h in range(-1, height + 1):
            if 0 <= h < height:
                at = f * chans * height + h
                value = rows[pl.ds(at, chans, stride=height), :].astype(BF16)
            else:
                value = zero
            for a in range(3):
                place(a, f, h, value)
    for a in range(3):
        done = jnp.dot(left[a], pool, preferred_element_type=F32).astype(BF16)
        for f in range(frames):
            for t in range(steps):
                at = (f * steps + t) * chans
                for b in range(3):
                    to = (a * 3 + b) * chans
                    s_ref[f, to : to + chans, t * LANES : (t + 1) * LANES] = done[
                        at : at + chans, b * LANES : (b + 1) * LANES
                    ]
    for b in range(3):
        w0, w1, w2 = (sw_ref[a, b].astype(F32) for a in range(3))
        for j, value in enumerate((w0, w0 + w1, w1 + w2, w2)):
            wc_ref[b, j * chans : (j + 1) * chans, :] = value.astype(BF16)


def dot_nt(a, b):
    return lax.dot_general(a, b, (((1,), (1,)), ((), ())), preferred_element_type=F32)


def main_kernel(scale, count, *refs):
    pieces, rest = refs[:count], refs[count:]
    before_ref, after_ref, s_ref, p_ref, tw_ref, g_ref, keep_ref, send_ref, cells, part = rest
    me = lax.axis_index("chan")
    at_frame = lax.axis_index("frames")
    last = lax.axis_size("frames") - 1
    quarter, spots = pieces[0].shape
    channels = count * quarter
    has_before = jnp.where(at_frame > 0, 1.0, 0.0).astype(BF16)
    has_after = jnp.where(at_frame < last, 1.0, 0.0).astype(BF16)
    for k in range(count):
        at = partner(me, k, count)
        cells[0, at] = pieces[k][...]
        cells[1, at] = before_ref[k] * has_before
        cells[2, at] = after_ref[k] * has_after
    now = cells[0].reshape(channels, spots)
    before = cells[1].reshape(channels, spots)
    after = cells[2].reshape(channels, spots)
    w0, w1, w2 = tw_ref[0], tw_ref[1], tw_ref[2]
    dot = functools.partial(jnp.dot, preferred_element_type=F32)
    middle = dot(w1, now)
    g0 = ((dot(w0, now) + middle + dot(w2, before)) * 0.125).astype(BF16)
    g1 = ((dot(w2, now) + middle + dot(w0, after)) * 0.125).astype(BF16)
    g_ref[0] = g0
    g_ref[1] = g1
    both_p = p_ref[...].reshape(2 * quarter, spots)
    e_now, e_before, e_after = (dot_nt(both_p, c) for c in (now, before, after))
    e0, e1 = e_now[:quarter], e_now[quarter:]
    small = scale * 0.125
    taps = s_ref.shape[1] // quarter
    spatial = (dot_nt(s_ref[0], g0) + dot_nt(s_ref[1], g1)) * scale
    part[:taps] = spatial.reshape(taps, quarter, channels)
    part[taps] = (e0 + e_after[quarter:]) * small
    part[taps + 1] = (e0 + e1) * small
    part[taps + 2] = (e_before[:quarter] + e1) * small
    half = part.shape[0] // 2
    side = lax.rem(at_frame, 2)
    keep_ref[...] = part[pl.ds(side * half, half)]
    send_ref[...] = part[pl.ds((1 - side) * half, half)]


def back_kernel(g_ref, wc_ref, out_ref, sums, rows):
    frames, chans, height, cols = out_ref.shape
    spread = one_hot_spread(cols)
    pooled = height // 2
    for f in range(frames):
        for t in range(height // 4):
            wide = jnp.dot(
                g_ref[f, :, t * LANES : (t + 1) * LANES], spread, preferred_element_type=F32
            ).astype(BF16)
            total = jnp.dot(wc_ref[0], wide[:, : 2 * cols], preferred_element_type=F32)
            for b in (1, 2):
                total = total + jnp.dot(
                    wc_ref[b],
                    wide[:, b * 2 * cols : (b + 1) * 2 * cols],
                    preferred_element_type=F32,
                )
            sums[2 * t] = total[:, :cols]
            sums[2 * t + 1] = total[:, cols:]
        for p in range(pooled):
            even = sums[p, chans : 2 * chans, :]
            if p > 0:
                even = even + sums[p - 1, 3 * chans :, :]
            odd = sums[p, 2 * chans : 3 * chans, :]
            if p < pooled - 1:
                odd = odd + sums[p + 1, :chans, :]
            rows[pl.ds(2 * p, chans, stride=height), :] = even
            rows[pl.ds(2 * p + 1, chans, stride=height), :] = odd
        out_ref[f] = rows[...].reshape(chans, height, cols).astype(BF16)


def partner(me, k, count):
    if count & (count - 1) == 0:
        return jnp.bitwise_xor(me, k)
    return lax.rem(me + k, count)


def swap(value, axis, k):
    count = lax.axis_size(axis)
    if count & (count - 1) == 0:
        pairs = [(i, i ^ k) for i in range(count)]
    else:
        pairs = [((i + k) % count, i) for i in range(count)]
    return lax.ppermute(value, axis, pairs)


def vmem(count):
    return [pl.BlockSpec(memory_space=pltpu.VMEM)] * count


def shape(dims, dtype):
    return jax.ShapeDtypeStruct(dims, dtype)


def cost(flops, size):
    return pl.CostEstimate(flops=flops, bytes_accessed=size, transcendentals=0)


def both(a, b):
    return a.astype(F32) + b.astype(F32)


def reduce_frames(keep, send):
    count = lax.axis_size("frames")
    side = lax.rem(lax.axis_index("frames"), 2)
    total = keep + swap(send, "frames", 1)
    bits = [1 << i for i in range(1, count.bit_length() - 1)]
    cut = total.shape[0] // 2
    a, b = total[:cut], total[cut:]
    for first, second in zip(bits, bits[::-1]):
        a, b = a.astype(BF16), b.astype(BF16)
        a, b = both(a, swap(a, "frames", first)), both(b, swap(b, "frames", second))
    mine = jnp.concatenate([a, b])
    other = swap(mine, "frames", 1)
    return jnp.where(side == 0, mine, other), jnp.where(side == 0, other, mine)


def shards(inputs, saved, cotangent, spatial_w, temporal_w):
    frames, quarter, height, cols = inputs.shape
    channels = temporal_w.shape[1]
    spots = cotangent.shape[2]
    count = lax.axis_size("chan")
    ring = lax.axis_size("frames")
    scale = 1.0 / math.sqrt(frames * ring * height * cols)
    steps = height // 4
    taps = spatial_w.shape[0] * spatial_w.shape[1]

    mine = cotangent[0]
    pieces = [mine] + [swap(mine, "chan", k) for k in range(1, count)]
    gathered = jnp.stack(pieces)
    up = [(i, (i + 1) % ring) for i in range(ring)]
    before = lax.ppermute(gathered, "frames", up)
    after = lax.ppermute(gathered, "frames", [(j, i) for i, j in up])

    sums, pooled, combined = pl.pallas_call(
        prep_kernel,
        out_shape=(
            shape((frames, taps * quarter, spots), BF16),
            shape((frames, quarter, spots), BF16),
            shape((3, 4 * quarter, channels), BF16),
        ),
        in_specs=vmem(3),
        out_specs=tuple(vmem(3)),
        scratch_shapes=[
            pltpu.VMEM((frames * quarter * height, cols), F32),
            pltpu.VMEM((3, frames * steps * quarter, 4 * cols), BF16),
        ],
        compiler_params=pltpu.CompilerParams(vmem_limit_bytes=20 << 20),
        cost_estimate=cost(1 << 30, 4 << 20),
        name="prep",
    )(inputs, saved, spatial_w)

    slices = taps + 3
    grad, keep, send = pl.pallas_call(
        functools.partial(main_kernel, scale, count),
        out_shape=(
            shape((frames, channels, spots), BF16),
            shape((slices // 2, quarter, channels), F32),
            shape((slices // 2, quarter, channels), F32),
        ),
        in_specs=vmem(count + 5),
        out_specs=tuple(vmem(3)),
        scratch_shapes=[
            pltpu.VMEM((3, count, quarter, spots), BF16),
            pltpu.VMEM((slices, quarter, channels), F32),
        ],
        compiler_params=pltpu.CompilerParams(vmem_limit_bytes=20 << 20),
        cost_estimate=cost(1 << 30, 4 << 20),
        name="main",
    )(*pieces, before, after, sums, pooled, temporal_w)

    input_grad = pl.pallas_call(
        back_kernel,
        out_shape=shape(inputs.shape, BF16),
        in_specs=vmem(2),
        out_specs=vmem(1)[0],
        scratch_shapes=[
            pltpu.VMEM((height // 2, 4 * quarter, cols), F32),
            pltpu.VMEM((quarter * height, cols), F32),
        ],
        compiler_params=pltpu.CompilerParams(vmem_limit_bytes=20 << 20),
        cost_estimate=cost(3 << 30, 4 << 20),
        name="back",
    )(grad, combined)

    low, high = reduce_frames(keep, send)
    rest = taps - slices // 2
    spatial = jnp.concatenate([low, high[:rest]])
    return (input_grad, spatial.reshape(spatial_w.shape), high[rest:])


def solution(mesh):
    return jax.shard_map(
        shards,
        mesh=mesh,
        in_specs=(
            P("frames", "chan", None, None),
            P("frames", "chan", None, None),
            P("frames", "chan", None),
            P(None, None, "chan", None),
            P(),
        ),
        out_specs=(
            P("frames", "chan", None, None),
            P(None, None, "chan", None),
            P(None, "chan", None),
        ),
        check_vma=False,
    )
```

```python
import functools
import math

import jax
import jax.numpy as jnp
from jax import lax
from jax.experimental import pallas as pl
from jax.experimental.pallas import tpu as pltpu
from jax.sharding import PartitionSpec as P

F32, BF16 = jnp.float32, jnp.bfloat16
LANES = 128


def one_hot_pool(slots, shifts, cols):
    half = LANES // 2
    shape = (slots * cols, len(shifts) * LANES)
    row = lax.broadcasted_iota(jnp.int32, shape, 0)
    col = lax.broadcasted_iota(jnp.int32, shape, 1)
    slot, w = row // cols, row % cols
    which, lane = col // LANES, col % LANES
    first = 2 * (lane % half) + which + (shifts[0] - 1)
    hit = (slot // 2 == lane // half) & ((w == first) | (w == first + 1))
    return jnp.where(hit, 1.0, 0.0).astype(BF16)


def one_hot_spread(cols):
    half = LANES // 2
    shape = (LANES, 3 * 2 * cols)
    row = lax.broadcasted_iota(jnp.int32, shape, 0)
    col = lax.broadcasted_iota(jnp.int32, shape, 1)
    tap, pair, w = col // (2 * cols), (col // cols) % 2, col % cols
    at = w - tap + 1
    hit = (at >= 0) & (at < cols) & (row == pair * half + at // 2)
    return jnp.where(hit, 1.0, 0.0).astype(BF16)


def prep_kernel(x_hbm, y_hbm, sw_hbm, s_ref, p_ref, wc_ref, x_ref, y_ref, sw_ref, sem, rows, left):
    fetches = [
        pltpu.make_async_copy(src, dst, sem.at[i])
        for i, (src, dst) in enumerate(((y_hbm, y_ref), (x_hbm, x_ref), (sw_hbm, sw_ref)))
    ]
    for fetch in fetches:
        fetch.start()
    frames, chans, height, cols = x_ref.shape
    steps = height // 4
    zero = jnp.zeros((chans, cols), BF16)
    pool = one_hot_pool(4, (0, 1, 2), cols)

    def place(a, f, h, value):
        t, slot = (h - a + 1) // 4, (h - a + 1) % 4
        if 0 <= t < steps:
            at = (f * steps + t) * chans
            left[a, at : at + chans, slot * cols : (slot + 1) * cols] = value

    fetches[0].wait()
    rows[...] = y_ref[...].reshape(frames * chans * height, cols).astype(F32)
    for f in range(frames):
        for h in range(height):
            at = f * chans * height + h
            place(1, f, h, rows[pl.ds(at, chans, stride=height), :].astype(BF16))
    done = jnp.dot(left[1], pool[:, LANES : 2 * LANES], preferred_element_type=F32).astype(BF16)
    for f in range(frames):
        for t in range(steps):
            at = (f * steps + t) * chans
            p_ref[f, :, t * LANES : (t + 1) * LANES] = done[at : at + chans]

    fetches[1].wait()
    rows[...] = x_ref[...].reshape(frames * chans * height, cols).astype(F32)
    for f in range(frames):
        for h in range(-1, height + 1):
            if 0 <= h < height:
                at = f * chans * height + h
                value = rows[pl.ds(at, chans, stride=height), :].astype(BF16)
            else:
                value = zero
            for a in range(3):
                place(a, f, h, value)
    for a in range(3):
        done = jnp.dot(left[a], pool, preferred_element_type=F32).astype(BF16)
        for f in range(frames):
            for t in range(steps):
                at = (f * steps + t) * chans
                for b in range(3):
                    to = (a * 3 + b) * chans
                    s_ref[f, to : to + chans, t * LANES : (t + 1) * LANES] = done[
                        at : at + chans, b * LANES : (b + 1) * LANES
                    ]
    fetches[2].wait()
    for b in range(3):
        w0, w1, w2 = (sw_ref[a, b].astype(F32) for a in range(3))
        for j, value in enumerate((w0, w0 + w1, w1 + w2, w2)):
            wc_ref[b, j * chans : (j + 1) * chans, :] = value.astype(BF16)


def dot_nt(a, b):
    return lax.dot_general(a, b, (((1,), (1,)), ((), ())), preferred_element_type=F32)


def main_kernel(scale, count, *refs):
    pieces, rest = refs[:count], refs[count:]
    outer, inner, rest = rest[:2], rest[2:4], rest[4:]
    s_ref, p_ref, tw_ref, g_ref, keep_ref, send_ref, cells, part = rest
    me = lax.axis_index("chan")
    at_frame = lax.axis_index("frames")
    last = lax.axis_size("frames") - 1
    quarter, spots = pieces[0].shape
    channels = count * quarter
    side = lax.rem(at_frame, 2)
    has_outer = jnp.where((at_frame > 0) & (at_frame < last), 1.0, 0.0).astype(BF16)
    cut = outer[0].shape[0]
    for k in range(count):
        at = partner(me, k, count)
        cells[0, at] = pieces[k][...]
        cells[1 + side, at] = outer[k // cut][k % cut] * has_outer
        cells[2 - side, at] = inner[k // cut][k % cut]
    now = cells[0].reshape(channels, spots)
    before = cells[1].reshape(channels, spots)
    after = cells[2].reshape(channels, spots)
    w0, w1, w2 = tw_ref[0], tw_ref[1], tw_ref[2]
    dot = functools.partial(jnp.dot, preferred_element_type=F32)
    middle = dot(w1, now)
    g0 = ((dot(w0, now) + middle + dot(w2, before)) * 0.125).astype(BF16)
    g1 = ((dot(w2, now) + middle + dot(w0, after)) * 0.125).astype(BF16)
    g_ref[0] = g0
    g_ref[1] = g1
    both_p = p_ref[...].reshape(2 * quarter, spots)
    e_now, e_before, e_after = (dot_nt(both_p, c) for c in (now, before, after))
    e0, e1 = e_now[:quarter], e_now[quarter:]
    small = scale * 0.125
    taps = s_ref.shape[1] // quarter
    spatial = (dot_nt(s_ref[0], g0) + dot_nt(s_ref[1], g1)) * scale
    part[:taps] = spatial.reshape(taps, quarter, channels)
    part[taps] = (e0 + e_after[quarter:]) * small
    part[taps + 1] = (e0 + e1) * small
    part[taps + 2] = (e_before[:quarter] + e1) * small
    half = part.shape[0] // 2
    keep_ref[...] = part[pl.ds(side * half, half)]
    send_ref[...] = part[pl.ds((1 - side) * half, half)]


def back_kernel(g_ref, wc_ref, out_ref, sums, rows):
    frames, chans, height, cols = out_ref.shape
    spread = one_hot_spread(cols)
    pooled = height // 2
    for f in range(frames):
        for t in range(height // 4):
            wide = jnp.dot(
                g_ref[f, :, t * LANES : (t + 1) * LANES], spread, preferred_element_type=F32
            ).astype(BF16)
            total = jnp.dot(wc_ref[0], wide[:, : 2 * cols], preferred_element_type=F32)
            for b in (1, 2):
                total = total + jnp.dot(
                    wc_ref[b],
                    wide[:, b * 2 * cols : (b + 1) * 2 * cols],
                    preferred_element_type=F32,
                )
            sums[2 * t] = total[:, :cols]
            sums[2 * t + 1] = total[:, cols:]
        for p in range(pooled):
            even = sums[p, chans : 2 * chans, :]
            if p > 0:
                even = even + sums[p - 1, 3 * chans :, :]
            odd = sums[p, 2 * chans : 3 * chans, :]
            if p < pooled - 1:
                odd = odd + sums[p + 1, :chans, :]
            rows[pl.ds(2 * p, chans, stride=height), :] = even
            rows[pl.ds(2 * p + 1, chans, stride=height), :] = odd
        out_ref[f] = rows[...].reshape(chans, height, cols).astype(BF16)


def partner(me, k, count):
    if count & (count - 1) == 0:
        return jnp.bitwise_xor(me, k)
    return lax.rem(me + k, count)


def swap(value, axis, k):
    count = lax.axis_size(axis)
    if count & (count - 1) == 0:
        pairs = [(i, i ^ k) for i in range(count)]
    else:
        pairs = [((i + k) % count, i) for i in range(count)]
    return lax.ppermute(value, axis, pairs)


def vmem(count):
    return [pl.BlockSpec(memory_space=pltpu.VMEM)] * count


def shape(dims, dtype):
    return jax.ShapeDtypeStruct(dims, dtype)


def cost(flops, size):
    return pl.CostEstimate(flops=flops, bytes_accessed=size, transcendentals=0)


def both(a, b):
    return a.astype(F32) + b.astype(F32)


def prep(inputs, saved, spatial_w):
    frames, quarter, height, cols = inputs.shape
    taps = spatial_w.shape[0] * spatial_w.shape[1]
    channels = spatial_w.shape[3]
    steps, spots = height // 4, height * cols // 4
    return pl.pallas_call(
        prep_kernel,
        out_shape=(
            shape((frames, taps * quarter, spots), BF16),
            shape((frames, quarter, spots), BF16),
            shape((3, 4 * quarter, channels), BF16),
        ),
        in_specs=[pl.BlockSpec(memory_space=pl.ANY)] * 3,
        out_specs=tuple(vmem(3)),
        scratch_shapes=[
            pltpu.VMEM(inputs.shape, BF16),
            pltpu.VMEM(inputs.shape, BF16),
            pltpu.VMEM(spatial_w.shape, BF16),
            pltpu.SemaphoreType.DMA((3,)),
            pltpu.VMEM((frames * quarter * height, cols), F32),
            pltpu.VMEM((3, frames * steps * quarter, 4 * cols), BF16),
        ],
        compiler_params=pltpu.CompilerParams(vmem_limit_bytes=20 << 20),
        cost_estimate=cost(1 << 30, 4 << 20),
        name="prep",
    )(inputs, saved, spatial_w)


def reduce_frames(keep, send, beside):
    count = lax.axis_size("frames")
    side = lax.rem(lax.axis_index("frames"), 2)
    total = keep + swap(send, "frames", 1)
    bits = [1 << i for i in range(1, count.bit_length() - 1)]
    cut = total.shape[0] // 2
    a, b = total[:cut], total[cut:]
    for first, second in zip(bits, bits[::-1]):
        a, b = a.astype(BF16), b.astype(BF16)
        a, b = both(a, swap(a, "frames", first)), both(b, swap(b, "frames", second))
        a, b, beside = lax.optimization_barrier((a, b, beside))
    mine = jnp.concatenate([a, b])
    other = swap(mine, "frames", 1)
    return jnp.where(side == 0, mine, other), jnp.where(side == 0, other, mine), beside


def shards(inputs, saved, cotangent, spatial_w, temporal_w):
    frames, quarter, height, cols = inputs.shape
    channels = temporal_w.shape[1]
    spots = cotangent.shape[2]
    count = lax.axis_size("chan")
    ring = lax.axis_size("frames")
    scale = 1.0 / math.sqrt(frames * ring * height * cols)
    taps = spatial_w.shape[0] * spatial_w.shape[1]

    pieces = [cotangent[0]]
    pieces += [swap(pieces[0], "chan", k) for k in range(1, count)]
    cut = count // 2
    parts = [jnp.stack(pieces[:cut]), jnp.stack(pieces[cut:])]
    across = [(i, (i + (1 if i % 2 else -1)) % ring) for i in range(ring)]
    other_chip = lax.ppermute(parts[0], "frames", across)
    sums, pooled, combined = prep(inputs, saved, spatial_w)
    parts[1], sums, pooled = lax.optimization_barrier((parts[1], sums, pooled))
    outer = [other_chip, lax.ppermute(parts[1], "frames", across)]
    inner = [swap(part, "frames", 1) for part in parts]

    slices = taps + 3
    grad, keep, send = pl.pallas_call(
        functools.partial(main_kernel, scale, count),
        out_shape=(
            shape((frames, channels, spots), BF16),
            shape((slices // 2, quarter, channels), F32),
            shape((slices // 2, quarter, channels), F32),
        ),
        in_specs=vmem(count + 7),
        out_specs=tuple(vmem(3)),
        scratch_shapes=[
            pltpu.VMEM((3, count, quarter, spots), BF16),
            pltpu.VMEM((slices, quarter, channels), F32),
        ],
        compiler_params=pltpu.CompilerParams(vmem_limit_bytes=20 << 20),
        cost_estimate=cost(1 << 30, 4 << 20),
        name="main",
    )(*pieces, *outer, *inner, sums, pooled, temporal_w)

    input_grad = pl.pallas_call(
        back_kernel,
        out_shape=shape(inputs.shape, BF16),
        in_specs=vmem(2),
        out_specs=vmem(1)[0],
        scratch_shapes=[
            pltpu.VMEM((height // 2, 4 * quarter, cols), F32),
            pltpu.VMEM((quarter * height, cols), F32),
        ],
        compiler_params=pltpu.CompilerParams(vmem_limit_bytes=20 << 20),
        cost_estimate=cost(3 << 30, 4 << 20),
        name="back",
    )(grad, combined)

    low, high, input_grad = reduce_frames(keep, send, input_grad)
    rest = taps - slices // 2
    spatial = jnp.concatenate([low, high[:rest]])
    return (input_grad, spatial.reshape(spatial_w.shape), high[rest:])


def solution(mesh):
    return jax.shard_map(
        shards,
        mesh=mesh,
        in_specs=(
            P("frames", "chan", None, None),
            P("frames", "chan", None, None),
            P("frames", "chan", None),
            P(None, None, "chan", None),
            P(),
        ),
        out_specs=(
            P("frames", "chan", None, None),
            P(None, None, "chan", None),
            P(None, "chan", None),
        ),
        check_vma=False,
    )
```

```python
import functools
import math

import jax
import jax.numpy as jnp
from jax import lax
from jax.experimental import pallas as pl
from jax.experimental.pallas import tpu as pltpu
from jax.sharding import PartitionSpec as P


F32, BF16 = jnp.float32, jnp.bfloat16
LANES = 128


def one_hot_pool(slots, shifts, cols):
    half = LANES // 2
    shape = (slots * cols, len(shifts) * LANES)
    row = lax.broadcasted_iota(jnp.int32, shape, 0)
    col = lax.broadcasted_iota(jnp.int32, shape, 1)
    slot, w = row // cols, row % cols
    which, lane = col // LANES, col % LANES
    first = 2 * (lane % half) + which + (shifts[0] - 1)
    hit = (slot // 2 == lane // half) & ((w == first) | (w == first + 1))
    return jnp.where(hit, 1.0, 0.0).astype(BF16)


def one_hot_spread(cols):
    half = LANES // 2
    shape = (LANES, 3 * 2 * cols)
    row = lax.broadcasted_iota(jnp.int32, shape, 0)
    col = lax.broadcasted_iota(jnp.int32, shape, 1)
    tap, pair, w = col // (2 * cols), (col // cols) % 2, col % cols
    at = w - tap + 1
    hit = (at >= 0) & (at < cols) & (row == pair * half + at // 2)
    return jnp.where(hit, 1.0, 0.0).astype(BF16)


def prep_kernel(x_hbm, y_hbm, sw_hbm, s_ref, p_ref, wc_ref, x_ref, y_ref, sw_ref, sem, rows, left):
    fetches = [
        pltpu.make_async_copy(src, dst, sem.at[i])
        for i, (src, dst) in enumerate(((y_hbm, y_ref), (x_hbm, x_ref), (sw_hbm, sw_ref)))
    ]
    for fetch in fetches:
        fetch.start()
    frames, chans, height, cols = x_ref.shape
    steps = height // 4
    zero = jnp.zeros((chans, cols), BF16)
    pool = one_hot_pool(4, (0, 1, 2), cols)

    def place(a, f, h, value):
        t, slot = (h - a + 1) // 4, (h - a + 1) % 4
        if 0 <= t < steps:
            at = (f * steps + t) * chans
            left[a, at : at + chans, slot * cols : (slot + 1) * cols] = value

    fetches[0].wait()
    rows[...] = y_ref[...].reshape(frames * chans * height, cols).astype(F32)
    for f in range(frames):
        for h in range(height):
            at = f * chans * height + h
            place(1, f, h, rows[pl.ds(at, chans, stride=height), :].astype(BF16))
    done = jnp.dot(left[1], pool[:, LANES : 2 * LANES], preferred_element_type=F32).astype(BF16)
    for f in range(frames):
        for t in range(steps):
            at = (f * steps + t) * chans
            p_ref[f, :, t * LANES : (t + 1) * LANES] = done[at : at + chans]

    fetches[1].wait()
    rows[...] = x_ref[...].reshape(frames * chans * height, cols).astype(F32)
    for f in range(frames):
        for h in range(-1, height + 1):
            if 0 <= h < height:
                at = f * chans * height + h
                value = rows[pl.ds(at, chans, stride=height), :].astype(BF16)
            else:
                value = zero
            for a in range(3):
                place(a, f, h, value)
    for a in range(3):
        done = jnp.dot(left[a], pool, preferred_element_type=F32).astype(BF16)
        for f in range(frames):
            for t in range(steps):
                at = (f * steps + t) * chans
                for b in range(3):
                    to = (a * 3 + b) * chans
                    s_ref[f, to : to + chans, t * LANES : (t + 1) * LANES] = done[
                        at : at + chans, b * LANES : (b + 1) * LANES
                    ]
    fetches[2].wait()
    for b in range(3):
        w0, w1, w2 = (sw_ref[a, b].astype(F32) for a in range(3))
        for j, value in enumerate((w0, w0 + w1, w1 + w2, w2)):
            wc_ref[b, j * chans : (j + 1) * chans, :] = value.astype(BF16)


def dot_nt(a, b):
    return lax.dot_general(a, b, (((1,), (1,)), ((), ())), preferred_element_type=F32)


def near_kernel(scale, count, *refs):
    pieces, inner, rest = refs[:count], refs[count : 2 * count], refs[2 * count :]
    s_ref, p_ref, tw_ref, base_ref, g_ref, part_ref, cells = rest
    side = lax.rem(lax.axis_index("frames"), 2)
    me = lax.axis_index("chan")
    quarter, spots = pieces[0].shape
    channels = count * quarter
    for k in range(count):
        at = partner(me, k, count)
        cells[0, at] = pieces[k][...]
        cells[1, at] = inner[k][...]
    now = cells[0].reshape(channels, spots)
    near = cells[1].reshape(channels, spots)
    dot = functools.partial(jnp.dot, preferred_element_type=F32)
    middle = dot(tw_ref[1], now)
    base_ref[...] = middle + dot(tw_ref[2 * side], now)
    g = middle + dot(tw_ref[2 - 2 * side], now) + dot(tw_ref[2 * side], near)
    g = (g * 0.125).astype(BF16)
    g_ref[...] = g
    pairs = p_ref[...].reshape(2 * quarter, spots)
    e_now, e_near = dot_nt(pairs, now), dot_nt(pairs, near)
    e0, e1 = e_now[:quarter], e_now[quarter:]
    small = scale * 0.125
    taps = s_ref.shape[1] // quarter
    part_ref[:taps] = (dot_nt(s_ref[1 - side], g) * scale).reshape(taps, quarter, channels)
    part_ref[taps] = e0 * small
    part_ref[taps + 1] = (e0 + e1) * small
    part_ref[taps + 2] = e1 * small
    first = jnp.where(side == 0, e_near[quarter:], e_near[:quarter]) * small
    part_ref[taps + 2 * side] += first


def far_kernel(scale, count, *refs):
    outer, rest = refs[:count], refs[count:]
    base_ref, part_ref, s_ref, p_ref, tw_ref, g_ref, keep_ref, send_ref, cells, part = rest
    at_frame = lax.axis_index("frames")
    side = lax.rem(at_frame, 2)
    me = lax.axis_index("chan")
    last = lax.axis_size("frames") - 1
    quarter, spots = outer[0].shape
    channels = count * quarter
    inside = jnp.where((at_frame > 0) & (at_frame < last), 1.0, 0.0).astype(BF16)
    for k in range(count):
        cells[partner(me, k, count)] = outer[k][...] * inside
    far = cells[...].reshape(channels, spots)
    g = base_ref[...] + jnp.dot(tw_ref[2 - 2 * side], far, preferred_element_type=F32)
    g = (g * 0.125).astype(BF16)
    g_ref[...] = g
    e_far = dot_nt(p_ref[...].reshape(2 * quarter, spots), far)
    taps = s_ref.shape[1] // quarter
    spatial = (dot_nt(s_ref[side], g) * scale).reshape(taps, quarter, channels)
    part[:taps] = part_ref[:taps] + spatial
    part[taps:] = part_ref[taps:]
    part[taps + 2 - 2 * side] += jnp.where(side == 0, e_far[:quarter], e_far[quarter:]) * (
        scale * 0.125
    )
    half = part.shape[0] // 2
    keep_ref[...] = part[pl.ds(side * half, half)]
    send_ref[...] = part[pl.ds((1 - side) * half, half)]


def finish_kernel(mine_ref, other_ref, spatial_hbm, temporal_hbm, sem):
    side = lax.rem(lax.axis_index("frames"), 2)
    half = mine_ref.shape[0]
    rest = spatial_hbm.shape[0] - half

    def copy_out(low, high):
        copies = [
            pltpu.make_async_copy(low, spatial_hbm.at[:half], sem.at[0]),
            pltpu.make_async_copy(high.at[:rest], spatial_hbm.at[half:], sem.at[1]),
            pltpu.make_async_copy(high.at[rest:], temporal_hbm, sem.at[2]),
        ]
        for copy in copies:
            copy.start()
        for copy in copies:
            copy.wait()

    @pl.when(side == 0)
    def _():
        copy_out(mine_ref, other_ref)

    @pl.when(side == 1)
    def _():
        copy_out(other_ref, mine_ref)


def back_kernel(near_ref, far_ref, wc_ref, out_ref, g_ref, sums, rows):
    frames, chans, height, cols = out_ref.shape
    side = lax.rem(lax.axis_index("frames"), 2)
    g_ref[1 - side] = near_ref[...]
    g_ref[side] = far_ref[...]
    spread = one_hot_spread(cols)
    pooled = height // 2
    for f in range(frames):
        for t in range(height // 4):
            wide = jnp.dot(
                g_ref[f, :, t * LANES : (t + 1) * LANES], spread, preferred_element_type=F32
            ).astype(BF16)
            total = jnp.dot(wc_ref[0], wide[:, : 2 * cols], preferred_element_type=F32)
            for b in (1, 2):
                total = total + jnp.dot(
                    wc_ref[b],
                    wide[:, b * 2 * cols : (b + 1) * 2 * cols],
                    preferred_element_type=F32,
                )
            sums[2 * t] = total[:, :cols]
            sums[2 * t + 1] = total[:, cols:]
        for p in range(pooled):
            even = sums[p, chans : 2 * chans, :]
            if p > 0:
                even = even + sums[p - 1, 3 * chans :, :]
            odd = sums[p, 2 * chans : 3 * chans, :]
            if p < pooled - 1:
                odd = odd + sums[p + 1, :chans, :]
            rows[pl.ds(2 * p, chans, stride=height), :] = even
            rows[pl.ds(2 * p + 1, chans, stride=height), :] = odd
        out_ref[f] = rows[...].reshape(chans, height, cols).astype(BF16)


def partner(me, k, count):
    if count & (count - 1) == 0:
        return jnp.bitwise_xor(me, k)
    return lax.rem(me + k, count)


def swap(value, axis, k):
    count = lax.axis_size(axis)
    if count & (count - 1) == 0:
        pairs = [(i, i ^ k) for i in range(count)]
    else:
        pairs = [((i + k) % count, i) for i in range(count)]
    return lax.ppermute(value, axis, pairs)


def vmem(count):
    return [pl.BlockSpec(memory_space=pltpu.VMEM)] * count


def shape(dims, dtype):
    return jax.ShapeDtypeStruct(dims, dtype)


def cost(flops, size):
    return pl.CostEstimate(flops=flops, bytes_accessed=size, transcendentals=0)


def both(a, b):
    return a.astype(F32) + b.astype(F32)


def prep(inputs, saved, spatial_w):
    frames, quarter, height, cols = inputs.shape
    taps = spatial_w.shape[0] * spatial_w.shape[1]
    channels = spatial_w.shape[3]
    steps, spots = height // 4, height * cols // 4
    return pl.pallas_call(
        prep_kernel,
        out_shape=(
            shape((frames, taps * quarter, spots), BF16),
            shape((frames, quarter, spots), BF16),
            shape((3, 4 * quarter, channels), BF16),
        ),
        in_specs=[pl.BlockSpec(memory_space=pltpu.HBM)] * 3,
        out_specs=tuple(vmem(3)),
        scratch_shapes=[
            pltpu.VMEM(inputs.shape, BF16),
            pltpu.VMEM(inputs.shape, BF16),
            pltpu.VMEM(spatial_w.shape, BF16),
            pltpu.SemaphoreType.DMA((3,)),
            pltpu.VMEM((frames * quarter * height, cols), F32),
            pltpu.VMEM((3, frames * steps * quarter, 4 * cols), BF16),
        ],
        compiler_params=pltpu.CompilerParams(vmem_limit_bytes=20 << 20),
        cost_estimate=cost(1 << 30, 4 << 20),
        name="prep",
    )(inputs, saved, spatial_w)


def reduce_frames(keep, send):
    count = lax.axis_size("frames")
    total = keep + swap(send, "frames", 1)
    bits = [1 << i for i in range(1, count.bit_length() - 1)]
    cut = total.shape[0] // 2
    a, b = total[:cut], total[cut:]
    for first, second in zip(bits, bits[::-1]):
        a, b = a.astype(BF16), b.astype(BF16)
        moved_a = swap(a, "frames", first)
        moved_b = swap(b, "frames", second)
        a, b = both(a, moved_a), both(b, moved_b)
    mine = jnp.concatenate([a, b])
    return mine, swap(mine, "frames", 1)


def shards(inputs, saved, cotangent, spatial_w, temporal_w):
    frames, quarter, height, cols = inputs.shape
    channels = temporal_w.shape[1]
    spots = cotangent.shape[2]
    count = lax.axis_size("chan")
    ring = lax.axis_size("frames")
    scale = 1.0 / math.sqrt(frames * ring * height * cols)
    taps = spatial_w.shape[0] * spatial_w.shape[1]

    pieces = [cotangent[0]]
    pieces += [swap(pieces[0], "chan", k) for k in range(1, count)]
    across = [(i, (i + (1 if i % 2 else -1)) % ring) for i in range(ring)]
    held = (pltpu.with_memory_space_constraint(x, pltpu.HBM) for x in (inputs, saved, spatial_w))
    sums, pooled, combined = prep(*held)
    outer = [lax.ppermute(piece, "frames", across) for piece in pieces]
    inner = [swap(piece, "frames", 1) for piece in pieces]

    slices = taps + 3
    limit = pltpu.CompilerParams(vmem_limit_bytes=20 << 20)
    part_shape = shape((slices, quarter, channels), F32)
    half_shape = shape((slices // 2, quarter, channels), F32)
    base, g_near, part = pl.pallas_call(
        functools.partial(near_kernel, scale, count),
        out_shape=(shape((channels, spots), F32), shape((channels, spots), BF16), part_shape),
        in_specs=vmem(2 * count + 3),
        out_specs=tuple(vmem(3)),
        scratch_shapes=[pltpu.VMEM((2, count, quarter, spots), BF16)],
        compiler_params=limit,
        cost_estimate=cost(1 << 30, 4 << 20),
        name="near",
    )(*pieces, *inner, sums, pooled, temporal_w)
    g_far, keep, send = pl.pallas_call(
        functools.partial(far_kernel, scale, count),
        out_shape=(shape((channels, spots), BF16), half_shape, half_shape),
        in_specs=vmem(count + 5),
        out_specs=tuple(vmem(3)),
        scratch_shapes=[
            pltpu.VMEM((count, quarter, spots), BF16),
            pltpu.VMEM(part_shape.shape, F32),
        ],
        compiler_params=limit,
        cost_estimate=cost(1 << 29, 4 << 20),
        name="far",
    )(*outer, base, part, sums, pooled, temporal_w)

    input_grad = pl.pallas_call(
        back_kernel,
        out_shape=shape(inputs.shape, BF16),
        in_specs=vmem(3),
        out_specs=vmem(1)[0],
        scratch_shapes=[
            pltpu.VMEM((frames, channels, spots), BF16),
            pltpu.VMEM((height // 2, 4 * quarter, cols), F32),
            pltpu.VMEM((quarter * height, cols), F32),
        ],
        compiler_params=limit,
        cost_estimate=cost(3 << 30, 4 << 20),
        name="back",
    )(g_near, g_far, combined)

    spatial, temporal = pl.pallas_call(
        finish_kernel,
        out_shape=(
            shape((taps, quarter, channels), F32),
            shape((slices - taps, quarter, channels), F32),
        ),
        in_specs=vmem(2),
        out_specs=(pl.BlockSpec(memory_space=pltpu.HBM),) * 2,
        scratch_shapes=[pltpu.SemaphoreType.DMA((3,))],
        compiler_params=limit,
        cost_estimate=cost(0, 4 << 20),
        name="finish",
    )(*reduce_frames(keep, send))
    return (input_grad, spatial.reshape(spatial_w.shape), temporal)


def solution(mesh):
    return jax.shard_map(
        shards,
        mesh=mesh,
        in_specs=(
            P("frames", "chan", None, None),
            P("frames", "chan", None, None),
            P("frames", "chan", None),
            P(None, None, "chan", None),
            P(),
        ),
        out_specs=(
            P("frames", "chan", None, None),
            P(None, None, "chan", None),
            P(None, "chan", None),
        ),
        check_vma=False,
    )
```

```python
import functools
import math

import jax
import jax.numpy as jnp
from jax import lax
from jax.experimental import pallas as pl
from jax.experimental.pallas import tpu as pltpu
from jax.sharding import PartitionSpec as P


F32, BF16 = jnp.float32, jnp.bfloat16
LANES = 128


def one_hot_pool(slots, shifts, cols):
    half = LANES // 2
    shape = (slots * cols, len(shifts) * LANES)
    row = lax.broadcasted_iota(jnp.int32, shape, 0)
    col = lax.broadcasted_iota(jnp.int32, shape, 1)
    slot, w = row // cols, row % cols
    which, lane = col // LANES, col % LANES
    first = 2 * (lane % half) + which + (shifts[0] - 1)
    hit = (slot // 2 == lane // half) & ((w == first) | (w == first + 1))
    return jnp.where(hit, 1.0, 0.0).astype(BF16)


def one_hot_spread(cols):
    half = LANES // 2
    shape = (LANES, 3 * 2 * cols)
    row = lax.broadcasted_iota(jnp.int32, shape, 0)
    col = lax.broadcasted_iota(jnp.int32, shape, 1)
    tap, pair, w = col // (2 * cols), (col // cols) % 2, col % cols
    at = w - tap + 1
    hit = (at >= 0) & (at < cols) & (row == pair * half + at // 2)
    return jnp.where(hit, 1.0, 0.0).astype(BF16)


def relayout(src, rows, left, windows):
    frames, chans, height, cols = src.shape
    steps = height // 4
    zero = jnp.zeros((chans, cols), BF16)
    rows[...] = src[...].reshape(frames * chans * height, cols).astype(F32)
    for f in range(frames):
        for h in range(-1, height + 1):
            value = zero
            if 0 <= h < height:
                at = f * chans * height + h
                value = rows[pl.ds(at, chans, stride=height), :].astype(BF16)
            for i, start in enumerate(windows):
                t, slot = (h - start) // 4, (h - start) % 4
                if 0 <= t < steps:
                    at = (f * steps + t) * chans
                    left[i, at : at + chans, slot * cols : (slot + 1) * cols] = value


def saved_kernel(x_hbm, y_hbm, sw_hbm, p_ref, x_ref, sw_ref, y_ref, sem, rows, left):
    frames, chans, height, cols = y_ref.shape
    steps = height // 4
    fetches = [
        pltpu.make_async_copy(src, dst, sem.at[i])
        for i, (src, dst) in enumerate(((y_hbm, y_ref), (x_hbm, x_ref), (sw_hbm, sw_ref)))
    ]
    for fetch in fetches:
        fetch.start()
    pool = one_hot_pool(4, (1,), cols)
    fetches[0].wait()
    relayout(y_ref, rows, left, (0,))
    done = jnp.dot(left[0], pool, preferred_element_type=F32).astype(BF16)
    for f in range(frames):
        for t in range(steps):
            at = (f * steps + t) * chans
            p_ref[f, :, t * LANES : (t + 1) * LANES] = done[at : at + chans]
    fetches[1].wait()
    fetches[2].wait()


def input_kernel(x_ref, s_ref, rows, left):
    frames, chans, height, cols = x_ref.shape
    steps = height // 4
    pool = one_hot_pool(4, (0, 1, 2), cols)
    relayout(x_ref, rows, left, (-1, 0, 1))
    for a in range(3):
        done = jnp.dot(left[a], pool, preferred_element_type=F32).astype(BF16)
        for f in range(frames):
            for t in range(steps):
                at = (f * steps + t) * chans
                for b in range(3):
                    to = (a * 3 + b) * chans
                    s_ref[f, to : to + chans, t * LANES : (t + 1) * LANES] = done[
                        at : at + chans, b * LANES : (b + 1) * LANES
                    ]


def dot_nt(a, b):
    return lax.dot_general(a, b, (((1,), (1,)), ((), ())), preferred_element_type=F32)


def piece_of(refs, place):
    return refs[place[0]][...] if place[1] is None else refs[place[0]][place[1]]


def near_kernel(scale, count, order, sent, *refs):
    pieces, inner, rest = refs[:count], refs[count : count + sent], refs[count + sent :]
    s_ref, p_ref, tw_ref, base_ref, g_ref, part_ref, cells = rest
    side = lax.rem(lax.axis_index("frames"), 2)
    me = lax.axis_index("chan")
    quarter, spots = pieces[0].shape
    channels = count * quarter
    for k in range(count):
        at = partner(me, k, count)
        cells[0, at] = pieces[k][...]
        cells[1, at] = piece_of(inner, order[k])
    now = cells[0].reshape(channels, spots)
    near = cells[1].reshape(channels, spots)
    dot = functools.partial(jnp.dot, preferred_element_type=F32)
    middle = dot(tw_ref[1], now)
    base_ref[...] = middle + dot(tw_ref[2 * side], now)
    g = middle + dot(tw_ref[2 - 2 * side], now) + dot(tw_ref[2 * side], near)
    g = (g * 0.125).astype(BF16)
    g_ref[...] = g
    pairs = p_ref[...].reshape(2 * quarter, spots)
    e_now, e_near = dot_nt(pairs, now), dot_nt(pairs, near)
    e0, e1 = e_now[:quarter], e_now[quarter:]
    small = scale * 0.125
    taps = s_ref.shape[1] // quarter
    part_ref[:taps] = (dot_nt(s_ref[1 - side], g) * scale).reshape(taps, quarter, channels)
    part_ref[taps] = e0 * small
    part_ref[taps + 1] = (e0 + e1) * small
    part_ref[taps + 2] = e1 * small
    first = jnp.where(side == 0, e_near[quarter:], e_near[:quarter]) * small
    part_ref[taps + 2 * side] += first


def far_kernel(scale, count, order, sent, *refs):
    outer, rest = refs[:sent], refs[sent:]
    base_ref, part_ref, s_ref, p_ref, tw_ref, g_ref, keep_ref, send_ref, cells, part = rest
    at_frame = lax.axis_index("frames")
    side = lax.rem(at_frame, 2)
    me = lax.axis_index("chan")
    last = lax.axis_size("frames") - 1
    quarter, spots = outer[0].shape
    channels = count * quarter
    inside = jnp.where((at_frame > 0) & (at_frame < last), 1.0, 0.0).astype(BF16)
    for k in range(count):
        cells[partner(me, k, count)] = piece_of(outer, order[k]) * inside
    far = cells[...].reshape(channels, spots)
    g = base_ref[...] + jnp.dot(tw_ref[2 - 2 * side], far, preferred_element_type=F32)
    g = (g * 0.125).astype(BF16)
    g_ref[...] = g
    e_far = dot_nt(p_ref[...].reshape(2 * quarter, spots), far)
    taps = s_ref.shape[1] // quarter
    spatial = (dot_nt(s_ref[side], g) * scale).reshape(taps, quarter, channels)
    part[:taps] = part_ref[:taps] + spatial
    part[taps:] = part_ref[taps:]
    part[taps + 2 - 2 * side] += jnp.where(side == 0, e_far[:quarter], e_far[quarter:]) * (
        scale * 0.125
    )
    half = part.shape[0] // 2
    keep_ref[...] = part[pl.ds(side * half, half)]
    send_ref[...] = part[pl.ds((1 - side) * half, half)]


def copy_half(low, half_ref, spatial_hbm, temporal_hbm, sem):
    half = half_ref.shape[0]
    rest = spatial_hbm.shape[0] - half

    @pl.when(low)
    def _():
        copy = pltpu.make_async_copy(half_ref, spatial_hbm.at[:half], sem.at[0])
        copy.start()
        copy.wait()

    @pl.when(jnp.logical_not(low))
    def _():
        copies = [
            pltpu.make_async_copy(half_ref.at[:rest], spatial_hbm.at[half:], sem.at[0]),
            pltpu.make_async_copy(half_ref.at[rest:], temporal_hbm, sem.at[1]),
        ]
        for copy in copies:
            copy.start()
        for copy in copies:
            copy.wait()


def early_kernel(mine_ref, spatial_hbm, temporal_hbm, sem):
    side = lax.rem(lax.axis_index("frames"), 2)
    copy_half(side == 0, mine_ref, spatial_hbm, temporal_hbm, sem)


def finish_kernel(other_ref, spatial_in, temporal_in, spatial_hbm, temporal_hbm, sem):
    side = lax.rem(lax.axis_index("frames"), 2)
    copy_half(side == 1, other_ref, spatial_hbm, temporal_hbm, sem)


def back_kernel(near_ref, far_ref, sw_ref, out_ref, g_ref, sums, rows, wc_ref):
    frames, chans, height, cols = out_ref.shape
    for b in range(3):
        w0, w1, w2 = (sw_ref[a, b].astype(F32) for a in range(3))
        for j, value in enumerate((w0, w0 + w1, w1 + w2, w2)):
            wc_ref[b, j * chans : (j + 1) * chans, :] = value.astype(BF16)
    side = lax.rem(lax.axis_index("frames"), 2)
    g_ref[1 - side] = near_ref[...]
    g_ref[side] = far_ref[...]
    spread = one_hot_spread(cols)
    pooled = height // 2
    for f in range(frames):
        for t in range(height // 4):
            wide = jnp.dot(
                g_ref[f, :, t * LANES : (t + 1) * LANES], spread, preferred_element_type=F32
            ).astype(BF16)
            total = jnp.dot(wc_ref[0], wide[:, : 2 * cols], preferred_element_type=F32)
            for b in (1, 2):
                total = total + jnp.dot(
                    wc_ref[b],
                    wide[:, b * 2 * cols : (b + 1) * 2 * cols],
                    preferred_element_type=F32,
                )
            sums[2 * t] = total[:, :cols]
            sums[2 * t + 1] = total[:, cols:]
        for p in range(pooled):
            even = sums[p, chans : 2 * chans, :]
            if p > 0:
                even = even + sums[p - 1, 3 * chans :, :]
            odd = sums[p, 2 * chans : 3 * chans, :]
            if p < pooled - 1:
                odd = odd + sums[p + 1, :chans, :]
            rows[pl.ds(2 * p, chans, stride=height), :] = even
            rows[pl.ds(2 * p + 1, chans, stride=height), :] = odd
        out_ref[f] = rows[...].reshape(chans, height, cols).astype(BF16)


def partner(me, k, count):
    if count & (count - 1) == 0:
        return jnp.bitwise_xor(me, k)
    return lax.rem(me + k, count)


def swap(value, axis, k):
    count = lax.axis_size(axis)
    if count & (count - 1) == 0:
        pairs = [(i, i ^ k) for i in range(count)]
    else:
        pairs = [((i + k) % count, i) for i in range(count)]
    return lax.ppermute(value, axis, pairs)


def vmem(count):
    return [pl.BlockSpec(memory_space=pltpu.VMEM)] * count


def shape(dims, dtype):
    return jax.ShapeDtypeStruct(dims, dtype)


def cost(flops, size):
    return pl.CostEstimate(flops=flops, bytes_accessed=size, transcendentals=0)


def both(a, b):
    return a.astype(F32) + b.astype(F32)


def prep(inputs, saved, spatial_w):
    frames, quarter, height, cols = inputs.shape
    taps = spatial_w.shape[0] * spatial_w.shape[1]
    groups, spots = frames * height // 4 * quarter, height * cols // 4
    rows = pltpu.VMEM((frames * quarter * height, cols), F32)
    limit = pltpu.CompilerParams(vmem_limit_bytes=20 << 20)
    held = [pltpu.with_memory_space_constraint(x, pltpu.HBM) for x in (inputs, saved, spatial_w)]
    pooled, staged, weights = pl.pallas_call(
        saved_kernel,
        out_shape=(
            shape((frames, quarter, spots), BF16),
            shape(inputs.shape, BF16),
            shape(spatial_w.shape, BF16),
        ),
        in_specs=[pl.BlockSpec(memory_space=pltpu.HBM)] * 3,
        out_specs=tuple(vmem(3)),
        scratch_shapes=[
            pltpu.VMEM(inputs.shape, BF16),
            pltpu.SemaphoreType.DMA((3,)),
            rows,
            pltpu.VMEM((1, groups, 4 * cols), BF16),
        ],
        compiler_params=limit,
        cost_estimate=cost(1 << 29, 4 << 20),
        name="prep_saved",
    )(*held)
    sums = pl.pallas_call(
        input_kernel,
        out_shape=shape((frames, taps * quarter, spots), BF16),
        in_specs=vmem(1),
        out_specs=vmem(1)[0],
        scratch_shapes=[rows, pltpu.VMEM((3, groups, 4 * cols), BF16)],
        compiler_params=limit,
        cost_estimate=cost(1 << 30, 4 << 20),
        name="prep_inputs",
    )(staged)
    return sums, pooled, weights


def reduce_frames(keep, send):
    count = lax.axis_size("frames")
    total = keep + swap(send, "frames", 1)
    bits = [1 << i for i in range(1, count.bit_length() - 1)]
    cut = total.shape[0] // 2
    a, b = total[:cut], total[cut:]
    for first, second in zip(bits, bits[::-1]):
        a, b = a.astype(BF16), b.astype(BF16)
        moved_a = swap(a, "frames", first)
        moved_b = swap(b, "frames", second)
        a, b = both(a, moved_a), both(b, moved_b)
    mine = jnp.concatenate([a, b])
    return mine, swap(mine, "frames", 1)


def shards(inputs, saved, cotangent, spatial_w, temporal_w):
    frames, quarter, height, cols = inputs.shape
    channels = temporal_w.shape[1]
    spots = cotangent.shape[2]
    count = lax.axis_size("chan")
    ring = lax.axis_size("frames")
    scale = 1.0 / math.sqrt(frames * ring * height * cols)
    taps = spatial_w.shape[0] * spatial_w.shape[1]

    pieces = [cotangent[0]]
    pieces += [swap(pieces[0], "chan", k) for k in range(1, count)]
    across = [(i, (i + (1 if i % 2 else -1)) % ring) for i in range(ring)]
    sums, pooled, weights = prep(inputs, saved, spatial_w)
    groups = [[k] for k in range(count)]
    order = {k: (i, j if len(g) > 1 else None) for i, g in enumerate(groups) for j, k in enumerate(g)}
    outer, inner = [], []
    for group in groups:
        value = pieces[group[0]] if len(group) == 1 else jnp.stack([pieces[k] for k in group])
        outer.append(lax.ppermute(value, "frames", across))
        inner.append(swap(value, "frames", 1))

    slices = taps + 3
    limit = pltpu.CompilerParams(vmem_limit_bytes=20 << 20)
    part_shape = shape((slices, quarter, channels), F32)
    half_shape = shape((slices // 2, quarter, channels), F32)
    base, g_near, part = pl.pallas_call(
        functools.partial(near_kernel, scale, count, order, len(inner)),
        out_shape=(shape((channels, spots), F32), shape((channels, spots), BF16), part_shape),
        in_specs=vmem(count + len(inner) + 3),
        out_specs=tuple(vmem(3)),
        scratch_shapes=[pltpu.VMEM((2, count, quarter, spots), BF16)],
        compiler_params=limit,
        cost_estimate=cost(1 << 30, 4 << 20),
        name="near",
    )(*pieces, *inner, sums, pooled, temporal_w)
    g_far, keep, send = pl.pallas_call(
        functools.partial(far_kernel, scale, count, order, len(outer)),
        out_shape=(shape((channels, spots), BF16), half_shape, half_shape),
        in_specs=vmem(len(outer) + 5),
        out_specs=tuple(vmem(3)),
        scratch_shapes=[
            pltpu.VMEM((count, quarter, spots), BF16),
            pltpu.VMEM(part_shape.shape, F32),
        ],
        compiler_params=limit,
        cost_estimate=cost(1 << 29, 4 << 20),
        name="far",
    )(*outer, base, part, sums, pooled, temporal_w)

    input_grad = pl.pallas_call(
        back_kernel,
        out_shape=shape(inputs.shape, BF16),
        in_specs=vmem(3),
        out_specs=vmem(1)[0],
        scratch_shapes=[
            pltpu.VMEM((frames, channels, spots), BF16),
            pltpu.VMEM((height // 2, 4 * quarter, cols), F32),
            pltpu.VMEM((quarter * height, cols), F32),
            pltpu.VMEM((3, 4 * quarter, channels), BF16),
        ],
        compiler_params=limit,
        cost_estimate=cost(3 << 30, 4 << 20),
        name="back",
    )(g_near, g_far, weights)

    mine, other = reduce_frames(keep, send)
    sums_out = dict(
        out_shape=(
            shape((taps, quarter, channels), F32),
            shape((slices - taps, quarter, channels), F32),
        ),
        out_specs=(pl.BlockSpec(memory_space=pltpu.HBM),) * 2,
        scratch_shapes=[pltpu.SemaphoreType.DMA((2,))],
        compiler_params=limit,
        cost_estimate=cost(0, 4 << 20),
    )
    begun = pl.pallas_call(early_kernel, in_specs=vmem(1), name="early", **sums_out)(mine)
    spatial, temporal = pl.pallas_call(
        finish_kernel,
        in_specs=vmem(1) + [pl.BlockSpec(memory_space=pltpu.HBM)] * 2,
        input_output_aliases={1: 0, 2: 1},
        name="finish",
        **sums_out,
    )(other, *begun)
    return (input_grad, spatial.reshape(spatial_w.shape), temporal)


def solution(mesh):
    return jax.shard_map(
        shards,
        mesh=mesh,
        in_specs=(
            P("frames", "chan", None, None),
            P("frames", "chan", None, None),
            P("frames", "chan", None),
            P(None, None, "chan", None),
            P(),
        ),
        out_specs=(
            P("frames", "chan", None, None),
            P(None, None, "chan", None),
            P(None, "chan", None),
        ),
        check_vma=False,
    )
```

```python
import functools
import math

import jax
import jax.numpy as jnp
from jax import lax
from jax.experimental import pallas as pl
from jax.experimental.pallas import tpu as pltpu
from jax.sharding import PartitionSpec as P


F32, BF16 = jnp.float32, jnp.bfloat16
LANES = 128


def one_hot_pool(slots, shifts, cols):
    half = LANES // 2
    shape = (slots * cols, len(shifts) * LANES)
    row = lax.broadcasted_iota(jnp.int32, shape, 0)
    col = lax.broadcasted_iota(jnp.int32, shape, 1)
    slot, w = row // cols, row % cols
    which, lane = col // LANES, col % LANES
    first = 2 * (lane % half) + which + (shifts[0] - 1)
    hit = (slot // 2 == lane // half) & ((w == first) | (w == first + 1))
    return jnp.where(hit, 1.0, 0.0).astype(BF16)


def one_hot_spread(cols):
    half = LANES // 2
    shape = (LANES, 3 * 2 * cols)
    row = lax.broadcasted_iota(jnp.int32, shape, 0)
    col = lax.broadcasted_iota(jnp.int32, shape, 1)
    tap, pair, w = col // (2 * cols), (col // cols) % 2, col % cols
    at = w - tap + 1
    hit = (at >= 0) & (at < cols) & (row == pair * half + at // 2)
    return jnp.where(hit, 1.0, 0.0).astype(BF16)


def relayout(src, rows, left, windows):
    frames, chans, height, cols = src.shape
    steps = height // 4
    zero = jnp.zeros((chans, cols), BF16)
    rows[...] = src[...].reshape(frames * chans * height, cols).astype(F32)
    for f in range(frames):
        for h in range(-1, height + 1):
            value = zero
            if 0 <= h < height:
                at = f * chans * height + h
                value = rows[pl.ds(at, chans, stride=height), :].astype(BF16)
            for i, start in enumerate(windows):
                t, slot = (h - start) // 4, (h - start) % 4
                if 0 <= t < steps:
                    at = (f * steps + t) * chans
                    left[i, at : at + chans, slot * cols : (slot + 1) * cols] = value


def saved_kernel(x_hbm, y_hbm, sw_hbm, p_ref, x_ref, sw_ref, y_ref, sem, rows, left):
    frames, chans, height, cols = y_ref.shape
    steps = height // 4
    fetches = [
        pltpu.make_async_copy(src, dst, sem.at[i])
        for i, (src, dst) in enumerate(((y_hbm, y_ref), (x_hbm, x_ref), (sw_hbm, sw_ref)))
    ]
    for fetch in fetches:
        fetch.start()
    pool = one_hot_pool(4, (1,), cols)
    fetches[0].wait()
    relayout(y_ref, rows, left, (0,))
    done = jnp.dot(left[0], pool, preferred_element_type=F32).astype(BF16)
    for f in range(frames):
        for t in range(steps):
            at = (f * steps + t) * chans
            p_ref[f, :, t * LANES : (t + 1) * LANES] = done[at : at + chans]
    fetches[1].wait()
    fetches[2].wait()


def input_kernel(x_ref, s_ref, rows, left):
    frames, chans, height, cols = x_ref.shape
    steps = height // 4
    pool = one_hot_pool(4, (0, 1, 2), cols)
    relayout(x_ref, rows, left, (-1, 0, 1))
    for a in range(3):
        done = jnp.dot(left[a], pool, preferred_element_type=F32).astype(BF16)
        for f in range(frames):
            for t in range(steps):
                at = (f * steps + t) * chans
                for b in range(3):
                    to = (a * 3 + b) * chans
                    s_ref[f, to : to + chans, t * LANES : (t + 1) * LANES] = done[
                        at : at + chans, b * LANES : (b + 1) * LANES
                    ]


def dot_nt(a, b):
    return lax.dot_general(a, b, (((1,), (1,)), ((), ())), preferred_element_type=F32)


def piece_of(refs, place):
    return refs[place[0]][...] if place[1] is None else refs[place[0]][place[1]]


def near_kernel(scale, count, order, sent, *refs):
    pieces, inner, rest = refs[:count], refs[count : count + sent], refs[count + sent :]
    s_ref, p_ref, tw_ref, base_ref, g_ref, part_ref, cells = rest
    side = lax.rem(lax.axis_index("frames"), 2)
    me = lax.axis_index("chan")
    quarter, spots = pieces[0].shape
    channels = count * quarter
    for k in range(count):
        at = partner(me, k, count)
        cells[0, at] = pieces[k][...]
        cells[1, at] = piece_of(inner, order[k])
    now = cells[0].reshape(channels, spots)
    near = cells[1].reshape(channels, spots)
    dot = functools.partial(jnp.dot, preferred_element_type=F32)
    middle = dot(tw_ref[1], now)
    base_ref[...] = middle + dot(tw_ref[2 * side], now)
    g = middle + dot(tw_ref[2 - 2 * side], now) + dot(tw_ref[2 * side], near)
    g = (g * 0.125).astype(BF16)
    g_ref[...] = g
    pairs = p_ref[...].reshape(2 * quarter, spots)
    e_now, e_near = dot_nt(pairs, now), dot_nt(pairs, near)
    e0, e1 = e_now[:quarter], e_now[quarter:]
    small = scale * 0.125
    taps = s_ref.shape[1] // quarter
    part_ref[:taps] = (dot_nt(s_ref[1 - side], g) * scale).reshape(taps, quarter, channels)
    part_ref[taps] = e0 * small
    part_ref[taps + 1] = (e0 + e1) * small
    part_ref[taps + 2] = e1 * small
    first = jnp.where(side == 0, e_near[quarter:], e_near[:quarter]) * small
    part_ref[taps + 2 * side] += first


def add_half(low, a_ref, b_ref, scale, part_ref, s_ref, p_ref, g, far):
    side = lax.rem(lax.axis_index("frames"), 2)
    cut, quarter, channels = a_ref.shape
    half = cut + b_ref.shape[0]
    edge = half * quarter
    taps = s_ref.shape[1] // quarter
    rows = s_ref[side, :edge] if low else s_ref[side, edge:]
    spatial = (dot_nt(rows, g) * scale).reshape(-1, quarter, channels)
    first = 0 if low else half
    a_ref[...] = part_ref[first : first + cut] + spatial[:cut]
    if low:
        b_ref[...] = part_ref[cut:half] + spatial[cut:]
        return
    e_far = dot_nt(p_ref[...].reshape(2 * quarter, far.shape[1]), far) * (scale * 0.125)
    b_ref[...] = part_ref[taps:]
    b_ref[2 - 2 * side] += jnp.where(side == 0, e_far[:quarter], e_far[quarter:])


def far_kernel(scale, count, order, sent, *refs):
    outer, rest = refs[:sent], refs[sent:]
    base_ref, part_ref, s_ref, p_ref, tw_ref, g_ref, send_a, send_b, cells_ref = rest
    at_frame = lax.axis_index("frames")
    side = lax.rem(at_frame, 2)
    me = lax.axis_index("chan")
    last = lax.axis_size("frames") - 1
    quarter, spots = outer[0].shape
    inside = jnp.where((at_frame > 0) & (at_frame < last), 1.0, 0.0).astype(BF16)
    for k in range(count):
        cells_ref[partner(me, k, count)] = piece_of(outer, order[k]) * inside
    far = cells_ref[...].reshape(count * quarter, spots)
    g = base_ref[...] + jnp.dot(tw_ref[2 - 2 * side], far, preferred_element_type=F32)
    g = (g * 0.125).astype(BF16)
    g_ref[...] = g
    for low in (True, False):

        @pl.when(side == int(low))
        def _(low=low):
            add_half(low, send_a, send_b, scale, part_ref, s_ref, p_ref, g_ref[...], far)


def keep_kernel(scale, part_ref, s_ref, p_ref, g_ref, cells_ref, keep_a, keep_b):
    side = lax.rem(lax.axis_index("frames"), 2)
    count, quarter, spots = cells_ref.shape
    for low in (True, False):

        @pl.when(side == 1 - int(low))
        def _(low=low):
            far = cells_ref[...].reshape(count * quarter, spots)
            add_half(low, keep_a, keep_b, scale, part_ref, s_ref, p_ref, g_ref[...], far)


def early_kernel(a_ref, b_ref, other_a, spatial_hbm, temporal_hbm, sem):
    side = lax.rem(lax.axis_index("frames"), 2)
    cut, half = a_ref.shape[0], a_ref.shape[0] + b_ref.shape[0]

    def copy_out(*moves):
        copies = [pltpu.make_async_copy(*move, sem.at[i]) for i, move in enumerate(moves)]
        for copy in copies:
            copy.start()
        for copy in copies:
            copy.wait()

    low, high = spatial_hbm.at[:cut], spatial_hbm.at[half:]

    @pl.when(side == 0)
    def _():
        copy_out((a_ref, low), (b_ref, spatial_hbm.at[cut:half]), (other_a, high))

    @pl.when(side == 1)
    def _():
        copy_out((a_ref, high), (b_ref, temporal_hbm), (other_a, low))


def finish_kernel(b_ref, spatial_in, temporal_in, spatial_hbm, temporal_hbm, sem):
    side = lax.rem(lax.axis_index("frames"), 2)
    rest = b_ref.shape[0]
    cut = spatial_hbm.shape[0] - 2 * rest

    def copy_out(to):
        copy = pltpu.make_async_copy(b_ref, to, sem.at[0])
        copy.start()
        copy.wait()

    @pl.when(side == 0)
    def _():
        copy_out(temporal_hbm)

    @pl.when(side == 1)
    def _():
        copy_out(spatial_hbm.at[cut : cut + rest])


def back_frame(g_ref, wc_ref, out_hbm, frame, sums, rows, staged, sem):
    chans, height, cols = staged.shape
    spread = one_hot_spread(cols)
    pooled = height // 2
    for t in range(height // 4):
        wide = jnp.dot(
            g_ref[:, t * LANES : (t + 1) * LANES], spread, preferred_element_type=F32
        ).astype(BF16)
        total = jnp.dot(wc_ref[0], wide[:, : 2 * cols], preferred_element_type=F32)
        for b in (1, 2):
            total = total + jnp.dot(
                wc_ref[b], wide[:, b * 2 * cols : (b + 1) * 2 * cols], preferred_element_type=F32
            )
        sums[2 * t] = total[:, :cols]
        sums[2 * t + 1] = total[:, cols:]
    for p in range(pooled):
        even = sums[p, chans : 2 * chans, :]
        if p > 0:
            even = even + sums[p - 1, 3 * chans :, :]
        odd = sums[p, 2 * chans : 3 * chans, :]
        if p < pooled - 1:
            odd = odd + sums[p + 1, :chans, :]
        rows[pl.ds(2 * p, chans, stride=height), :] = even
        rows[pl.ds(2 * p + 1, chans, stride=height), :] = odd
    staged[...] = rows[...].reshape(chans, height, cols).astype(BF16)
    copy = pltpu.make_async_copy(staged, out_hbm.at[frame], sem)
    copy.start()
    copy.wait()


def back_near_kernel(g_ref, sw_ref, out_hbm, wc_ref, *scratch):
    chans = sw_ref.shape[2]
    for b in range(3):
        w0, w1, w2 = (sw_ref[a, b].astype(F32) for a in range(3))
        for j, value in enumerate((w0, w0 + w1, w1 + w2, w2)):
            wc_ref[b, j * chans : (j + 1) * chans, :] = value.astype(BF16)
    side = lax.rem(lax.axis_index("frames"), 2)
    back_frame(g_ref, wc_ref, out_hbm, 1 - side, *scratch)


def back_far_kernel(g_ref, wc_ref, out_in, out_hbm, *scratch):
    side = lax.rem(lax.axis_index("frames"), 2)
    back_frame(g_ref, wc_ref, out_hbm, side, *scratch)


def partner(me, k, count):
    if count & (count - 1) == 0:
        return jnp.bitwise_xor(me, k)
    return lax.rem(me + k, count)


def swap(value, axis, k):
    count = lax.axis_size(axis)
    if count & (count - 1) == 0:
        pairs = [(i, i ^ k) for i in range(count)]
    else:
        pairs = [((i + k) % count, i) for i in range(count)]
    return lax.ppermute(value, axis, pairs)


def vmem(count):
    return [pl.BlockSpec(memory_space=pltpu.VMEM)] * count


def shape(dims, dtype):
    return jax.ShapeDtypeStruct(dims, dtype)


def cost(flops, size):
    return pl.CostEstimate(flops=flops, bytes_accessed=size, transcendentals=0)


def both(a, b):
    return a.astype(F32) + b.astype(F32)


def prep(inputs, saved, spatial_w):
    frames, quarter, height, cols = inputs.shape
    taps = spatial_w.shape[0] * spatial_w.shape[1]
    groups, spots = frames * height // 4 * quarter, height * cols // 4
    rows = pltpu.VMEM((frames * quarter * height, cols), F32)
    limit = pltpu.CompilerParams(vmem_limit_bytes=20 << 20)
    held = [pltpu.with_memory_space_constraint(x, pltpu.HBM) for x in (inputs, saved, spatial_w)]
    pooled, staged, weights = pl.pallas_call(
        saved_kernel,
        out_shape=(
            shape((frames, quarter, spots), BF16),
            shape(inputs.shape, BF16),
            shape(spatial_w.shape, BF16),
        ),
        in_specs=[pl.BlockSpec(memory_space=pltpu.HBM)] * 3,
        out_specs=tuple(vmem(3)),
        scratch_shapes=[
            pltpu.VMEM(inputs.shape, BF16),
            pltpu.SemaphoreType.DMA((3,)),
            rows,
            pltpu.VMEM((1, groups, 4 * cols), BF16),
        ],
        compiler_params=limit,
        cost_estimate=cost(1 << 29, 4 << 20),
        name="prep_saved",
    )(*held)
    sums = pl.pallas_call(
        input_kernel,
        out_shape=shape((frames, taps * quarter, spots), BF16),
        in_specs=vmem(1),
        out_specs=vmem(1)[0],
        scratch_shapes=[rows, pltpu.VMEM((3, groups, 4 * cols), BF16)],
        compiler_params=limit,
        cost_estimate=cost(1 << 30, 4 << 20),
        name="prep_inputs",
    )(staged)
    return sums, pooled, weights


def apart(value, other):
    return lax.optimization_barrier((value, other))[0]


def reduce_frames(keep, send):
    count = lax.axis_size("frames")
    bits = [1 << i for i in range(1, count.bit_length() - 1)]
    a, b = keep
    moved_a = swap(send[0], "frames", 1)
    moved_b = swap(send[1], "frames", 1)
    for first, second in zip(bits, bits[::-1]):
        a = both(a, moved_a).astype(BF16)
        b = both(b, apart(moved_b, a)).astype(BF16)
        moved_a = swap(a, "frames", first)
        moved_b = swap(b, "frames", second)
    a = both(a, moved_a)
    b = both(b, apart(moved_b, a))
    others = (swap(a, "frames", 1), swap(b, "frames", 1))
    return (a, b), others


def shards(inputs, saved, cotangent, spatial_w, temporal_w):
    frames, quarter, height, cols = inputs.shape
    channels = temporal_w.shape[1]
    spots = cotangent.shape[2]
    count = lax.axis_size("chan")
    ring = lax.axis_size("frames")
    scale = 1.0 / math.sqrt(frames * ring * height * cols)
    taps = spatial_w.shape[0] * spatial_w.shape[1]

    pieces = [cotangent[0]]
    pieces += [swap(pieces[0], "chan", k) for k in range(1, count)]
    across = [(i, (i + (1 if i % 2 else -1)) % ring) for i in range(ring)]
    sums, pooled, weights = prep(inputs, saved, spatial_w)
    groups = [[k] for k in range(count)]
    order = {k: (i, j if len(g) > 1 else None) for i, g in enumerate(groups) for j, k in enumerate(g)}
    outer, inner = [], []
    for group in groups:
        value = pieces[group[0]] if len(group) == 1 else jnp.stack([pieces[k] for k in group])
        outer.append(lax.ppermute(value, "frames", across))
        inner.append(swap(value, "frames", 1))

    slices = taps + 3
    limit = pltpu.CompilerParams(vmem_limit_bytes=20 << 20)
    part_shape = shape((slices, quarter, channels), F32)
    half_shapes = [shape((n, quarter, channels), F32) for n in (taps - slices // 2, slices - taps)]
    base, g_near, part = pl.pallas_call(
        functools.partial(near_kernel, scale, count, order, len(inner)),
        out_shape=(shape((channels, spots), F32), shape((channels, spots), BF16), part_shape),
        in_specs=vmem(count + len(inner) + 3),
        out_specs=tuple(vmem(3)),
        scratch_shapes=[pltpu.VMEM((2, count, quarter, spots), BF16)],
        compiler_params=limit,
        cost_estimate=cost(1 << 30, 4 << 20),
        name="near",
    )(*pieces, *inner, sums, pooled, temporal_w)
    g_far, send_a, send_b, cells = pl.pallas_call(
        functools.partial(far_kernel, scale, count, order, len(outer)),
        out_shape=(
            shape((channels, spots), BF16),
            *half_shapes,
            shape((count, quarter, spots), BF16),
        ),
        in_specs=vmem(len(outer) + 5),
        out_specs=tuple(vmem(4)),
        compiler_params=limit,
        cost_estimate=cost(1 << 29, 4 << 20),
        name="far",
    )(*outer, base, part, sums, pooled, temporal_w)
    keep = pl.pallas_call(
        functools.partial(keep_kernel, scale),
        out_shape=tuple(half_shapes),
        in_specs=vmem(5),
        out_specs=tuple(vmem(2)),
        compiler_params=limit,
        cost_estimate=cost(1 << 28, 4 << 20),
        name="keep",
    )(part, sums, pooled, g_far, cells)

    hbm = pl.BlockSpec(memory_space=pltpu.HBM)
    back = dict(
        scratch_shapes=[
            pltpu.VMEM((height // 2, 4 * quarter, cols), F32),
            pltpu.VMEM((quarter * height, cols), F32),
            pltpu.VMEM((quarter, height, cols), BF16),
            pltpu.SemaphoreType.DMA,
        ],
        compiler_params=limit,
        cost_estimate=cost(3 << 29, 2 << 20),
    )
    input_grad, combined = pl.pallas_call(
        back_near_kernel,
        out_shape=(shape(inputs.shape, BF16), shape((3, 4 * quarter, channels), BF16)),
        in_specs=vmem(2),
        out_specs=(hbm, *vmem(1)),
        name="back_near",
        **back,
    )(g_near, weights)
    input_grad = pl.pallas_call(
        back_far_kernel,
        out_shape=shape(inputs.shape, BF16),
        in_specs=[*vmem(2), hbm],
        out_specs=hbm,
        input_output_aliases={2: 0},
        name="back_far",
        **back,
    )(g_far, combined, input_grad)

    mine, other = reduce_frames(keep, (send_a, send_b))
    sums_out = dict(
        out_shape=(
            shape((taps, quarter, channels), F32),
            shape((slices - taps, quarter, channels), F32),
        ),
        out_specs=(pl.BlockSpec(memory_space=pltpu.HBM),) * 2,
        scratch_shapes=[pltpu.SemaphoreType.DMA((3,))],
        compiler_params=limit,
        cost_estimate=cost(0, 4 << 20),
    )
    begun = pl.pallas_call(early_kernel, in_specs=vmem(3), name="early", **sums_out)(*mine, other[0])
    spatial, temporal = pl.pallas_call(
        finish_kernel,
        in_specs=vmem(1) + [pl.BlockSpec(memory_space=pltpu.HBM)] * 2,
        input_output_aliases={1: 0, 2: 1},
        name="finish",
        **sums_out,
    )(other[1], *begun)
    return (input_grad, spatial.reshape(spatial_w.shape), temporal)


def solution(mesh):
    return jax.shard_map(
        shards,
        mesh=mesh,
        in_specs=(
            P("frames", "chan", None, None),
            P("frames", "chan", None, None),
            P("frames", "chan", None),
            P(None, None, "chan", None),
            P(),
        ),
        out_specs=(
            P("frames", "chan", None, None),
            P(None, None, "chan", None),
            P(None, "chan", None),
        ),
        check_vma=False,
    )
```

```python
import functools
import math

import jax
import jax.numpy as jnp
from jax import lax
from jax.experimental import pallas as pl
from jax.experimental.pallas import tpu as pltpu
from jax.sharding import PartitionSpec as P


F32, BF16 = jnp.float32, jnp.bfloat16
LANES = 128


def one_hot_pool(slots, shifts, cols):
    half = LANES // 2
    shape = (slots * cols, len(shifts) * LANES)
    row = lax.broadcasted_iota(jnp.int32, shape, 0)
    col = lax.broadcasted_iota(jnp.int32, shape, 1)
    slot, w = row // cols, row % cols
    which, lane = col // LANES, col % LANES
    first = 2 * (lane % half) + which + (shifts[0] - 1)
    hit = (slot // 2 == lane // half) & ((w == first) | (w == first + 1))
    return jnp.where(hit, 1.0, 0.0).astype(BF16)


def one_hot_spread(cols):
    half = LANES // 2
    shape = (LANES, 3 * 2 * cols)
    row = lax.broadcasted_iota(jnp.int32, shape, 0)
    col = lax.broadcasted_iota(jnp.int32, shape, 1)
    tap, pair, w = col // (2 * cols), (col // cols) % 2, col % cols
    at = w - tap + 1
    hit = (at >= 0) & (at < cols) & (row == pair * half + at // 2)
    return jnp.where(hit, 1.0, 0.0).astype(BF16)


def relayout(src, rows, left, windows):
    frames, chans, height, cols = src.shape
    steps = height // 4
    zero = jnp.zeros((chans, cols), BF16)
    rows[...] = src[...].reshape(frames * chans * height, cols).astype(F32)
    for f in range(frames):
        for h in range(-1, height + 1):
            value = zero
            if 0 <= h < height:
                at = f * chans * height + h
                value = rows[pl.ds(at, chans, stride=height), :].astype(BF16)
            for i, start in enumerate(windows):
                t, slot = (h - start) // 4, (h - start) % 4
                if 0 <= t < steps:
                    at = (f * steps + t) * chans
                    left[i, at : at + chans, slot * cols : (slot + 1) * cols] = value


def saved_kernel(
    x_hbm, y_hbm, sw_hbm, p_ref, x_ref, sw_ref, pool_ref, y_ref, sem, rows, left
):
    frames, chans, height, cols = y_ref.shape
    steps = height // 4
    fetches = [
        pltpu.make_async_copy(src, dst, sem.at[i])
        for i, (src, dst) in enumerate(((y_hbm, y_ref), (x_hbm, x_ref), (sw_hbm, sw_ref)))
    ]
    for fetch in fetches:
        fetch.start()
    pool_ref[...] = one_hot_pool(4, (0, 1, 2), cols)
    fetches[0].wait()
    relayout(y_ref, rows, left, (0,))
    middle = pool_ref[:, LANES : 2 * LANES]
    done = jnp.dot(left[0], middle, preferred_element_type=F32).astype(BF16)
    for f in range(frames):
        for t in range(steps):
            at = (f * steps + t) * chans
            p_ref[f, :, t * LANES : (t + 1) * LANES] = done[at : at + chans]
    fetches[1].wait()
    fetches[2].wait()


def input_kernel(x_ref, pool_ref, s_ref, rows, left):
    frames, chans, height, _ = x_ref.shape
    steps = height // 4
    relayout(x_ref, rows, left, (-1, 0, 1))
    for a in range(3):
        done = jnp.dot(left[a], pool_ref[...], preferred_element_type=F32).astype(BF16)
        for f in range(frames):
            for t in range(steps):
                at = (f * steps + t) * chans
                for b in range(3):
                    to = (a * 3 + b) * chans
                    s_ref[f, to : to + chans, t * LANES : (t + 1) * LANES] = done[
                        at : at + chans, b * LANES : (b + 1) * LANES
                    ]


def dot_nt(a, b):
    return lax.dot_general(a, b, (((1,), (1,)), ((), ())), preferred_element_type=F32)


def piece_of(refs, place):
    return refs[place[0]][...] if place[1] is None else refs[place[0]][place[1]]


def near_kernel(scale, count, order, sent, *refs):
    pieces, inner, rest = refs[:count], refs[count : count + sent], refs[count + sent :]
    s_ref, p_ref, tw_ref, base_ref, g_ref, sent_ref, temporal_ref, cells = rest
    side = lax.rem(lax.axis_index("frames"), 2)
    me = lax.axis_index("chan")
    quarter, spots = pieces[0].shape
    channels = count * quarter
    for k in range(count):
        at = partner(me, k, count)
        cells[0, at] = pieces[k][...]
        cells[1, at] = piece_of(inner, order[k])
    now = cells[0].reshape(channels, spots)
    near = cells[1].reshape(channels, spots)
    dot = functools.partial(jnp.dot, preferred_element_type=F32)
    taps_now = dot(tw_ref[...].reshape(3 * channels, channels), now)
    first, middle, third = (taps_now[k * channels : (k + 1) * channels] for k in range(3))
    base_ref[...] = middle + jnp.where(side == 0, first, third)
    g = middle + jnp.where(side == 0, third, first) + dot(tw_ref[2 * side], near)
    g = (g * 0.125).astype(BF16)
    g_ref[...] = g
    pairs = p_ref[...].reshape(2 * quarter, spots)
    e_now, e_near = dot_nt(pairs, now), dot_nt(pairs, near)
    e0, e1 = e_now[:quarter], e_now[quarter:]
    small = scale * 0.125
    temporal_ref[0] = e0 * small
    temporal_ref[1] = (e0 + e1) * small
    temporal_ref[2] = e1 * small
    temporal_ref[2 * side] += jnp.where(side == 0, e_near[quarter:], e_near[:quarter]) * small
    edge = sent_ref.shape[0] * quarter
    for low in (True, False):

        @pl.when(side == int(low))
        def _(low=low):
            spatial = dot_nt(half_rows(low, s_ref, 1 - side, edge), g_ref[...]) * scale
            spatial = spatial.reshape(-1, quarter, channels)
            sent_ref[: spatial.shape[0]] = spatial


def half_rows(low, s_ref, frame, edge):
    return s_ref[frame, :edge] if low else s_ref[frame, edge:]


def put_half(low, a_ref, b_ref, spatial, scale, temporal_ref, p_ref, far):
    cut, quarter, channels = a_ref.shape
    spatial = spatial.reshape(-1, quarter, channels)
    a_ref[...] = spatial[:cut]
    if low:
        b_ref[...] = spatial[cut:]
        return
    side = lax.rem(lax.axis_index("frames"), 2)
    e_far = dot_nt(p_ref[...].reshape(2 * quarter, far.shape[1]), far) * (scale * 0.125)
    b_ref[...] = temporal_ref[...]
    b_ref[2 - 2 * side] += jnp.where(side == 0, e_far[:quarter], e_far[quarter:])


def far_kernel(scale, count, order, sent, *refs):
    outer, rest = refs[:sent], refs[sent:]
    base_ref, sent_ref, temporal_ref, s_ref, p_ref, tw_ref = rest[:6]
    g_ref, send_a, send_b, cells_ref = rest[6:]
    at_frame = lax.axis_index("frames")
    side = lax.rem(at_frame, 2)
    me = lax.axis_index("chan")
    last = lax.axis_size("frames") - 1
    quarter, spots = outer[0].shape
    inside = jnp.where((at_frame > 0) & (at_frame < last), 1.0, 0.0).astype(BF16)
    for k in range(count):
        cells_ref[partner(me, k, count)] = piece_of(outer, order[k]) * inside
    far = cells_ref[...].reshape(count * quarter, spots)
    g = base_ref[...] + jnp.dot(tw_ref[2 - 2 * side], far, preferred_element_type=F32)
    g = (g * 0.125).astype(BF16)
    g_ref[...] = g
    for low in (True, False):

        @pl.when(side == int(low))
        def _(low=low):
            half, _, channels = sent_ref.shape
            spatial = dot_nt(half_rows(low, s_ref, side, half * quarter), g_ref[...]) * scale
            known = sent_ref[: spatial.shape[0] // quarter].reshape(-1, channels)
            put_half(low, send_a, send_b, known + spatial, scale, temporal_ref, p_ref, far)


def keep_kernel(
    scale, temporal_ref, s_ref, p_ref, near_ref, far_ref, cells_ref, keep_a, keep_b
):
    side = lax.rem(lax.axis_index("frames"), 2)
    count, quarter, spots = cells_ref.shape
    for low in (True, False):

        @pl.when(side == 1 - int(low))
        def _(low=low):
            far = cells_ref[...].reshape(count * quarter, spots)
            edge = (keep_a.shape[0] + keep_b.shape[0]) * quarter
            spatial = dot_nt(half_rows(low, s_ref, 1 - side, edge), near_ref[...])
            spatial += dot_nt(half_rows(low, s_ref, side, edge), far_ref[...])
            put_half(low, keep_a, keep_b, spatial * scale, scale, temporal_ref, p_ref, far)


def early_kernel(a_ref, b_ref, other_a, spatial_hbm, temporal_hbm, sem):
    side = lax.rem(lax.axis_index("frames"), 2)
    cut, half = a_ref.shape[0], a_ref.shape[0] + b_ref.shape[0]

    def copy_out(*moves):
        copies = [pltpu.make_async_copy(*move, sem.at[i]) for i, move in enumerate(moves)]
        for copy in copies:
            copy.start()
        for copy in copies:
            copy.wait()

    low, high = spatial_hbm.at[:cut], spatial_hbm.at[half:]

    @pl.when(side == 0)
    def _():
        copy_out((a_ref, low), (b_ref, spatial_hbm.at[cut:half]), (other_a, high))

    @pl.when(side == 1)
    def _():
        copy_out((a_ref, high), (b_ref, temporal_hbm), (other_a, low))


def finish_kernel(b_ref, spatial_in, temporal_in, spatial_hbm, temporal_hbm, sem):
    side = lax.rem(lax.axis_index("frames"), 2)
    rest = b_ref.shape[0]
    cut = spatial_hbm.shape[0] - 2 * rest

    def copy_out(to):
        copy = pltpu.make_async_copy(b_ref, to, sem.at[0])
        copy.start()
        copy.wait()

    @pl.when(side == 0)
    def _():
        copy_out(temporal_hbm)

    @pl.when(side == 1)
    def _():
        copy_out(spatial_hbm.at[cut : cut + rest])


def back_frame(g_ref, wc_ref, out_hbm, frame, sums, rows, staged, sem):
    chans, height, cols = staged.shape
    spread = one_hot_spread(cols)
    pooled = height // 2
    for t in range(height // 4):
        wide = jnp.dot(
            g_ref[:, t * LANES : (t + 1) * LANES], spread, preferred_element_type=F32
        ).astype(BF16)
        total = jnp.dot(wc_ref[0], wide[:, : 2 * cols], preferred_element_type=F32)
        for b in (1, 2):
            total = total + jnp.dot(
                wc_ref[b], wide[:, b * 2 * cols : (b + 1) * 2 * cols], preferred_element_type=F32
            )
        sums[2 * t] = total[:, :cols]
        sums[2 * t + 1] = total[:, cols:]
    for p in range(pooled):
        even = sums[p, chans : 2 * chans, :]
        if p > 0:
            even = even + sums[p - 1, 3 * chans :, :]
        odd = sums[p, 2 * chans : 3 * chans, :]
        if p < pooled - 1:
            odd = odd + sums[p + 1, :chans, :]
        rows[pl.ds(2 * p, chans, stride=height), :] = even
        rows[pl.ds(2 * p + 1, chans, stride=height), :] = odd
    staged[...] = rows[...].reshape(chans, height, cols).astype(BF16)
    copy = pltpu.make_async_copy(staged, out_hbm.at[frame], sem)
    copy.start()
    copy.wait()


def back_near_kernel(g_ref, sw_ref, out_hbm, wc_ref, *scratch):
    chans = sw_ref.shape[2]
    for b in range(3):
        w0, w1, w2 = (sw_ref[a, b].astype(F32) for a in range(3))
        for j, value in enumerate((w0, w0 + w1, w1 + w2, w2)):
            wc_ref[b, j * chans : (j + 1) * chans, :] = value.astype(BF16)
    side = lax.rem(lax.axis_index("frames"), 2)
    back_frame(g_ref, wc_ref, out_hbm, 1 - side, *scratch)


def back_far_kernel(g_ref, wc_ref, out_in, out_hbm, *scratch):
    side = lax.rem(lax.axis_index("frames"), 2)
    back_frame(g_ref, wc_ref, out_hbm, side, *scratch)


def partner(me, k, count):
    if count & (count - 1) == 0:
        return jnp.bitwise_xor(me, k)
    return lax.rem(me + k, count)


def swap(value, axis, k):
    count = lax.axis_size(axis)
    if count & (count - 1) == 0:
        pairs = [(i, i ^ k) for i in range(count)]
    else:
        pairs = [((i + k) % count, i) for i in range(count)]
    return lax.ppermute(value, axis, pairs)


def vmem(count):
    return [pl.BlockSpec(memory_space=pltpu.VMEM)] * count


def shape(dims, dtype):
    return jax.ShapeDtypeStruct(dims, dtype)


def cost(flops, size):
    return pl.CostEstimate(flops=flops, bytes_accessed=size, transcendentals=0)


def both(a, b):
    return a.astype(F32) + b.astype(F32)


def prep(inputs, saved, spatial_w):
    frames, quarter, height, cols = inputs.shape
    taps = spatial_w.shape[0] * spatial_w.shape[1]
    groups, spots = frames * height // 4 * quarter, height * cols // 4
    rows = pltpu.VMEM((frames * quarter * height, cols), F32)
    limit = pltpu.CompilerParams(vmem_limit_bytes=20 << 20)
    held = [pltpu.with_memory_space_constraint(x, pltpu.HBM) for x in (inputs, saved, spatial_w)]
    pooled, staged, weights, pool = pl.pallas_call(
        saved_kernel,
        out_shape=(
            shape((frames, quarter, spots), BF16),
            shape(inputs.shape, BF16),
            shape(spatial_w.shape, BF16),
            shape((4 * cols, 3 * LANES), BF16),
        ),
        in_specs=[pl.BlockSpec(memory_space=pltpu.HBM)] * 3,
        out_specs=tuple(vmem(4)),
        scratch_shapes=[
            pltpu.VMEM(inputs.shape, BF16),
            pltpu.SemaphoreType.DMA((3,)),
            rows,
            pltpu.VMEM((1, groups, 4 * cols), BF16),
        ],
        compiler_params=limit,
        cost_estimate=cost(1 << 29, 4 << 20),
        name="prep_saved",
    )(*held)
    sums = pl.pallas_call(
        input_kernel,
        out_shape=shape((frames, taps * quarter, spots), BF16),
        in_specs=vmem(2),
        out_specs=vmem(1)[0],
        scratch_shapes=[rows, pltpu.VMEM((3, groups, 4 * cols), BF16)],
        compiler_params=limit,
        cost_estimate=cost(1 << 30, 4 << 20),
        name="prep_inputs",
    )(staged, pool)
    return sums, pooled, weights


def apart(value, other):
    return lax.optimization_barrier((value, other))[0]


def reduce_frames(keep, send):
    count = lax.axis_size("frames")
    bits = [1 << i for i in range(1, count.bit_length() - 1)]
    a, b = keep
    moved_a = swap(send[0], "frames", 1)
    moved_b = swap(send[1], "frames", 1)
    for first, second in zip(bits, bits[::-1]):
        a = both(a, moved_a).astype(BF16)
        b = both(b, apart(moved_b, a)).astype(BF16)
        moved_a = swap(a, "frames", first)
        moved_b = swap(b, "frames", second)
    a = both(a, moved_a)
    b = both(b, apart(moved_b, a))
    others = (swap(a, "frames", 1), swap(b, "frames", 1))
    return (a, b), others


def shards(inputs, saved, cotangent, spatial_w, temporal_w):
    frames, quarter, height, cols = inputs.shape
    channels = temporal_w.shape[1]
    spots = cotangent.shape[2]
    count = lax.axis_size("chan")
    ring = lax.axis_size("frames")
    scale = 1.0 / math.sqrt(frames * ring * height * cols)
    taps = spatial_w.shape[0] * spatial_w.shape[1]

    pieces = [cotangent[0]]
    pieces += [swap(pieces[0], "chan", k) for k in range(1, count)]
    across = [(i, (i + (1 if i % 2 else -1)) % ring) for i in range(ring)]
    sums, pooled, weights = prep(inputs, saved, spatial_w)
    groups = [[k] for k in range(count)]
    order = {k: (i, j if len(g) > 1 else None) for i, g in enumerate(groups) for j, k in enumerate(g)}
    outer = []
    for group in groups:
        value = pieces[group[0]] if len(group) == 1 else jnp.stack([pieces[k] for k in group])
        if group == [1]:
            outer.append(swap(outer[0], "chan", 1))
        else:
            outer.append(lax.ppermute(value, "frames", across))

    near = [pieces[0], jnp.stack(pieces[1:])]
    inner = [swap(value, "frames", 1) for value in near]
    near_order = {k: (0, None) if k == 0 else (1, k - 1) for k in range(count)}

    slices = taps + 3
    limit = pltpu.CompilerParams(vmem_limit_bytes=20 << 20)
    half_shapes = [shape((n, quarter, channels), F32) for n in (taps - slices // 2, slices - taps)]
    base, g_near, sent, temporal_near = pl.pallas_call(
        functools.partial(near_kernel, scale, count, near_order, len(inner)),
        out_shape=(
            shape((channels, spots), F32),
            shape((channels, spots), BF16),
            shape((slices // 2, quarter, channels), F32),
            half_shapes[1],
        ),
        in_specs=vmem(count + len(inner) + 3),
        out_specs=tuple(vmem(4)),
        scratch_shapes=[pltpu.VMEM((2, count, quarter, spots), BF16)],
        compiler_params=limit,
        cost_estimate=cost(1 << 30, 4 << 20),
        name="near",
    )(*pieces, *inner, sums, pooled, temporal_w)
    g_far, send_a, send_b, cells = pl.pallas_call(
        functools.partial(far_kernel, scale, count, order, len(outer)),
        out_shape=(
            shape((channels, spots), BF16),
            *half_shapes,
            shape((count, quarter, spots), BF16),
        ),
        in_specs=vmem(len(outer) + 6),
        out_specs=tuple(vmem(4)),
        compiler_params=limit,
        cost_estimate=cost(1 << 29, 4 << 20),
        name="far",
    )(*outer, base, sent, temporal_near, sums, pooled, temporal_w)
    keep = pl.pallas_call(
        functools.partial(keep_kernel, scale),
        out_shape=tuple(half_shapes),
        in_specs=vmem(6),
        out_specs=tuple(vmem(2)),
        compiler_params=limit,
        cost_estimate=cost(1 << 28, 4 << 20),
        name="keep",
    )(temporal_near, sums, pooled, g_near, g_far, cells)

    hbm = pl.BlockSpec(memory_space=pltpu.HBM)
    back = dict(
        scratch_shapes=[
            pltpu.VMEM((height // 2, 4 * quarter, cols), F32),
            pltpu.VMEM((quarter * height, cols), F32),
            pltpu.VMEM((quarter, height, cols), BF16),
            pltpu.SemaphoreType.DMA,
        ],
        compiler_params=limit,
        cost_estimate=cost(3 << 29, 2 << 20),
    )
    input_grad, combined = pl.pallas_call(
        back_near_kernel,
        out_shape=(shape(inputs.shape, BF16), shape((3, 4 * quarter, channels), BF16)),
        in_specs=vmem(2),
        out_specs=(hbm, *vmem(1)),
        name="back_near",
        **back,
    )(g_near, weights)
    input_grad = pl.pallas_call(
        back_far_kernel,
        out_shape=shape(inputs.shape, BF16),
        in_specs=[*vmem(2), hbm],
        out_specs=hbm,
        input_output_aliases={2: 0},
        name="back_far",
        **back,
    )(g_far, combined, input_grad)

    mine, other = reduce_frames(keep, (send_a, send_b))
    sums_out = dict(
        out_shape=(
            shape((taps, quarter, channels), F32),
            shape((slices - taps, quarter, channels), F32),
        ),
        out_specs=(pl.BlockSpec(memory_space=pltpu.HBM),) * 2,
        scratch_shapes=[pltpu.SemaphoreType.DMA((3,))],
        compiler_params=limit,
        cost_estimate=cost(0, 4 << 20),
    )
    begun = pl.pallas_call(early_kernel, in_specs=vmem(3), name="early", **sums_out)(*mine, other[0])
    spatial, temporal = pl.pallas_call(
        finish_kernel,
        in_specs=vmem(1) + [pl.BlockSpec(memory_space=pltpu.HBM)] * 2,
        input_output_aliases={1: 0, 2: 1},
        name="finish",
        **sums_out,
    )(other[1], *begun)
    return (input_grad, spatial.reshape(spatial_w.shape), temporal)


def solution(mesh):
    return jax.shard_map(
        shards,
        mesh=mesh,
        in_specs=(
            P("frames", "chan", None, None),
            P("frames", "chan", None, None),
            P("frames", "chan", None),
            P(None, None, "chan", None),
            P(),
        ),
        out_specs=(
            P("frames", "chan", None, None),
            P(None, None, "chan", None),
            P(None, "chan", None),
        ),
        check_vma=False,
    )
```

```python
import functools
import math

import jax
import jax.numpy as jnp
from jax import lax
from jax.experimental import pallas as pl
from jax.experimental.pallas import tpu as pltpu
from jax.sharding import PartitionSpec as P


F32, BF16 = jnp.float32, jnp.bfloat16
LANES = 128


def one_hot_pool(slots, shifts, cols):
    half = LANES // 2
    shape = (slots * cols, len(shifts) * LANES)
    row = lax.broadcasted_iota(jnp.int32, shape, 0)
    col = lax.broadcasted_iota(jnp.int32, shape, 1)
    slot, w = row // cols, row % cols
    which, lane = col // LANES, col % LANES
    first = 2 * (lane % half) + which + (shifts[0] - 1)
    hit = (slot // 2 == lane // half) & ((w == first) | (w == first + 1))
    return jnp.where(hit, 1.0, 0.0).astype(BF16)


def one_hot_spread(cols):
    half = LANES // 2
    shape = (LANES, 3 * 2 * cols)
    row = lax.broadcasted_iota(jnp.int32, shape, 0)
    col = lax.broadcasted_iota(jnp.int32, shape, 1)
    tap, pair, w = col // (2 * cols), (col // cols) % 2, col % cols
    at = w - tap + 1
    hit = (at >= 0) & (at < cols) & (row == pair * half + at // 2)
    return jnp.where(hit, 1.0, 0.0).astype(BF16)


def relayout(src, rows, left, windows):
    frames, chans, height, cols = src.shape
    steps = height // 4
    zero = jnp.zeros((chans, cols), BF16)
    rows[...] = src[...].reshape(frames * chans * height, cols).astype(F32)
    for f in range(frames):
        for h in range(-1, height + 1):
            value = zero
            if 0 <= h < height:
                at = f * chans * height + h
                value = rows[pl.ds(at, chans, stride=height), :].astype(BF16)
            for i, start in enumerate(windows):
                t, slot = (h - start) // 4, (h - start) % 4
                if 0 <= t < steps:
                    at = (f * steps + t) * chans
                    left[i, at : at + chans, slot * cols : (slot + 1) * cols] = value


def saved_kernel(x_hbm, y_hbm, sw_hbm, p_ref, x_ref, sw_ref, y_ref, sem, rows, left):
    frames, chans, height, cols = y_ref.shape
    steps = height // 4
    fetches = [
        pltpu.make_async_copy(src, dst, sem.at[i])
        for i, (src, dst) in enumerate(((y_hbm, y_ref), (x_hbm, x_ref), (sw_hbm, sw_ref)))
    ]
    for fetch in fetches:
        fetch.start()
    pool = one_hot_pool(4, (1,), cols)
    fetches[0].wait()
    relayout(y_ref, rows, left, (0,))
    done = jnp.dot(left[0], pool, preferred_element_type=F32).astype(BF16)
    for f in range(frames):
        for t in range(steps):
            at = (f * steps + t) * chans
            p_ref[f, :, t * LANES : (t + 1) * LANES] = done[at : at + chans]
    fetches[1].wait()
    fetches[2].wait()


def input_kernel(x_ref, s_ref, rows, left):
    frames, chans, height, cols = x_ref.shape
    steps = height // 4
    pool = one_hot_pool(4, (0, 1, 2), cols)
    relayout(x_ref, rows, left, (-1, 0, 1))
    for a in range(3):
        done = jnp.dot(left[a], pool, preferred_element_type=F32).astype(BF16)
        for f in range(frames):
            for t in range(steps):
                at = (f * steps + t) * chans
                for b in range(3):
                    to = (a * 3 + b) * chans
                    s_ref[f, to : to + chans, t * LANES : (t + 1) * LANES] = done[
                        at : at + chans, b * LANES : (b + 1) * LANES
                    ]


def dot_nt(a, b):
    return lax.dot_general(a, b, (((1,), (1,)), ((), ())), preferred_element_type=F32)


def piece_of(refs, place):
    return refs[place[0]][...] if place[1] is None else refs[place[0]][place[1]]


def near_kernel(scale, count, order, sent, *refs):
    pieces, inner, rest = refs[:count], refs[count : count + sent], refs[count + sent :]
    s_ref, p_ref, tw_ref, base_ref, g_ref, part_ref, cells = rest
    side = lax.rem(lax.axis_index("frames"), 2)
    me = lax.axis_index("chan")
    quarter, spots = pieces[0].shape
    channels = count * quarter
    for k in range(count):
        at = partner(me, k, count)
        cells[0, at] = pieces[k][...]
        cells[1, at] = piece_of(inner, order[k])
    now = cells[0].reshape(channels, spots)
    near = cells[1].reshape(channels, spots)
    dot = functools.partial(jnp.dot, preferred_element_type=F32)
    middle = dot(tw_ref[1], now)
    base_ref[...] = middle + dot(tw_ref[2 * side], now)
    g = middle + dot(tw_ref[2 - 2 * side], now) + dot(tw_ref[2 * side], near)
    g = (g * 0.125).astype(BF16)
    g_ref[...] = g
    pairs = p_ref[...].reshape(2 * quarter, spots)
    e_now, e_near = dot_nt(pairs, now), dot_nt(pairs, near)
    e0, e1 = e_now[:quarter], e_now[quarter:]
    small = scale * 0.125
    taps = s_ref.shape[1] // quarter
    part_ref[:taps] = (dot_nt(s_ref[1 - side], g) * scale).reshape(taps, quarter, channels)
    part_ref[taps] = e0 * small
    part_ref[taps + 1] = (e0 + e1) * small
    part_ref[taps + 2] = e1 * small
    first = jnp.where(side == 0, e_near[quarter:], e_near[:quarter]) * small
    part_ref[taps + 2 * side] += first


def add_half(low, a_ref, b_ref, scale, part_ref, s_ref, p_ref, g, far):
    side = lax.rem(lax.axis_index("frames"), 2)
    cut, quarter, channels = a_ref.shape
    half = cut + b_ref.shape[0]
    edge = half * quarter
    taps = s_ref.shape[1] // quarter
    rows = s_ref[side, :edge] if low else s_ref[side, edge:]
    spatial = (dot_nt(rows, g) * scale).reshape(-1, quarter, channels)
    first = 0 if low else half
    a_ref[...] = part_ref[first : first + cut] + spatial[:cut]
    if low:
        b_ref[...] = part_ref[cut:half] + spatial[cut:]
        return
    e_far = dot_nt(p_ref[...].reshape(2 * quarter, far.shape[1]), far) * (scale * 0.125)
    b_ref[...] = part_ref[taps:]
    b_ref[2 - 2 * side] += jnp.where(side == 0, e_far[:quarter], e_far[quarter:])


def far_kernel(scale, count, order, sent, *refs):
    outer, rest = refs[:sent], refs[sent:]
    base_ref, part_ref, s_ref, p_ref, tw_ref, g_ref, send_a, send_b, cells_ref = rest
    at_frame = lax.axis_index("frames")
    side = lax.rem(at_frame, 2)
    me = lax.axis_index("chan")
    last = lax.axis_size("frames") - 1
    quarter, spots = outer[0].shape
    inside = jnp.where((at_frame > 0) & (at_frame < last), 1.0, 0.0).astype(BF16)
    for k in range(count):
        cells_ref[partner(me, k, count)] = piece_of(outer, order[k]) * inside
    far = cells_ref[...].reshape(count * quarter, spots)
    g = base_ref[...] + jnp.dot(tw_ref[2 - 2 * side], far, preferred_element_type=F32)
    g = (g * 0.125).astype(BF16)
    g_ref[...] = g
    for low in (True, False):

        @pl.when(side == int(low))
        def _(low=low):
            add_half(low, send_a, send_b, scale, part_ref, s_ref, p_ref, g_ref[...], far)


def keep_kernel(scale, part_ref, s_ref, p_ref, g_ref, cells_ref, keep_a, keep_b):
    side = lax.rem(lax.axis_index("frames"), 2)
    count, quarter, spots = cells_ref.shape
    for low in (True, False):

        @pl.when(side == 1 - int(low))
        def _(low=low):
            far = cells_ref[...].reshape(count * quarter, spots)
            add_half(low, keep_a, keep_b, scale, part_ref, s_ref, p_ref, g_ref[...], far)


def early_kernel(a_ref, b_ref, other_a, spatial_hbm, temporal_hbm, sem):
    side = lax.rem(lax.axis_index("frames"), 2)
    cut, half = a_ref.shape[0], a_ref.shape[0] + b_ref.shape[0]

    def copy_out(*moves):
        copies = [pltpu.make_async_copy(*move, sem.at[i]) for i, move in enumerate(moves)]
        for copy in copies:
            copy.start()
        for copy in copies:
            copy.wait()

    low, high = spatial_hbm.at[:cut], spatial_hbm.at[half:]

    @pl.when(side == 0)
    def _():
        copy_out((a_ref, low), (b_ref, spatial_hbm.at[cut:half]), (other_a, high))

    @pl.when(side == 1)
    def _():
        copy_out((a_ref, high), (b_ref, temporal_hbm), (other_a, low))


def finish_kernel(b_ref, spatial_in, temporal_in, spatial_hbm, temporal_hbm, sem):
    side = lax.rem(lax.axis_index("frames"), 2)
    rest = b_ref.shape[0]
    cut = spatial_hbm.shape[0] - 2 * rest

    def copy_out(to):
        copy = pltpu.make_async_copy(b_ref, to, sem.at[0])
        copy.start()
        copy.wait()

    @pl.when(side == 0)
    def _():
        copy_out(temporal_hbm)

    @pl.when(side == 1)
    def _():
        copy_out(spatial_hbm.at[cut : cut + rest])


def back_frame(g_ref, wc_ref, out_hbm, frame, sums, rows, staged, sem):
    chans, height, cols = staged.shape
    spread = one_hot_spread(cols)
    pooled = height // 2
    for t in range(height // 4):
        wide = jnp.dot(
            g_ref[:, t * LANES : (t + 1) * LANES], spread, preferred_element_type=F32
        ).astype(BF16)
        total = jnp.dot(wc_ref[0], wide[:, : 2 * cols], preferred_element_type=F32)
        for b in (1, 2):
            total = total + jnp.dot(
                wc_ref[b], wide[:, b * 2 * cols : (b + 1) * 2 * cols], preferred_element_type=F32
            )
        sums[2 * t] = total[:, :cols]
        sums[2 * t + 1] = total[:, cols:]
    for p in range(pooled):
        even = sums[p, chans : 2 * chans, :]
        if p > 0:
            even = even + sums[p - 1, 3 * chans :, :]
        odd = sums[p, 2 * chans : 3 * chans, :]
        if p < pooled - 1:
            odd = odd + sums[p + 1, :chans, :]
        rows[pl.ds(2 * p, chans, stride=height), :] = even
        rows[pl.ds(2 * p + 1, chans, stride=height), :] = odd
    staged[...] = rows[...].reshape(chans, height, cols).astype(BF16)
    copy = pltpu.make_async_copy(staged, out_hbm.at[frame], sem)
    copy.start()
    copy.wait()


def back_near_kernel(g_ref, sw_ref, out_hbm, wc_ref, *scratch):
    chans = sw_ref.shape[2]
    for b in range(3):
        w0, w1, w2 = (sw_ref[a, b].astype(F32) for a in range(3))
        for j, value in enumerate((w0, w0 + w1, w1 + w2, w2)):
            wc_ref[b, j * chans : (j + 1) * chans, :] = value.astype(BF16)
    side = lax.rem(lax.axis_index("frames"), 2)
    back_frame(g_ref, wc_ref, out_hbm, 1 - side, *scratch)


def back_far_kernel(g_ref, wc_ref, out_in, out_hbm, *scratch):
    side = lax.rem(lax.axis_index("frames"), 2)
    back_frame(g_ref, wc_ref, out_hbm, side, *scratch)


def partner(me, k, count):
    if count & (count - 1) == 0:
        return jnp.bitwise_xor(me, k)
    return lax.rem(me + k, count)


def swap(value, axis, k):
    count = lax.axis_size(axis)
    if count & (count - 1) == 0:
        pairs = [(i, i ^ k) for i in range(count)]
    else:
        pairs = [((i + k) % count, i) for i in range(count)]
    return lax.ppermute(value, axis, pairs)


def vmem(count):
    return [pl.BlockSpec(memory_space=pltpu.VMEM)] * count


def shape(dims, dtype):
    return jax.ShapeDtypeStruct(dims, dtype)


def cost(flops, size):
    return pl.CostEstimate(flops=flops, bytes_accessed=size, transcendentals=0)


def both(a, b):
    return a.astype(F32) + b.astype(F32)


def prep(inputs, saved, spatial_w):
    frames, quarter, height, cols = inputs.shape
    taps = spatial_w.shape[0] * spatial_w.shape[1]
    groups, spots = frames * height // 4 * quarter, height * cols // 4
    rows = pltpu.VMEM((frames * quarter * height, cols), F32)
    limit = pltpu.CompilerParams(vmem_limit_bytes=20 << 20)
    held = [pltpu.with_memory_space_constraint(x, pltpu.HBM) for x in (inputs, saved, spatial_w)]
    pooled, staged, weights = pl.pallas_call(
        saved_kernel,
        out_shape=(
            shape((frames, quarter, spots), BF16),
            shape(inputs.shape, BF16),
            shape(spatial_w.shape, BF16),
        ),
        in_specs=[pl.BlockSpec(memory_space=pltpu.HBM)] * 3,
        out_specs=tuple(vmem(3)),
        scratch_shapes=[
            pltpu.VMEM(inputs.shape, BF16),
            pltpu.SemaphoreType.DMA((3,)),
            rows,
            pltpu.VMEM((1, groups, 4 * cols), BF16),
        ],
        compiler_params=limit,
        cost_estimate=cost(1 << 29, 4 << 20),
        name="prep_saved",
    )(*held)
    sums = pl.pallas_call(
        input_kernel,
        out_shape=shape((frames, taps * quarter, spots), BF16),
        in_specs=vmem(1),
        out_specs=vmem(1)[0],
        scratch_shapes=[rows, pltpu.VMEM((3, groups, 4 * cols), BF16)],
        compiler_params=limit,
        cost_estimate=cost(1 << 30, 4 << 20),
        name="prep_inputs",
    )(staged)
    return sums, pooled, weights


def apart(value, other):
    return lax.optimization_barrier((value, other))[0]


def reduce_frames(keep, send):
    count = lax.axis_size("frames")
    bits = [1 << i for i in range(1, count.bit_length() - 1)]
    a, b = keep
    moved_a = swap(send[0], "frames", 1)
    moved_b = swap(send[1], "frames", 1)
    for first, second in zip(bits[::-1], bits):
        a = both(a, moved_a).astype(BF16)
        b = both(b, apart(moved_b, a)).astype(BF16)
        moved_a = swap(a, "frames", first)
        moved_b = swap(b, "frames", second)
    a = both(a, moved_a)
    b = both(b, apart(moved_b, a))
    others = (swap(a, "frames", 1), swap(b, "frames", 1))
    return (a, b), others


def shards(inputs, saved, cotangent, spatial_w, temporal_w):
    frames, quarter, height, cols = inputs.shape
    channels = temporal_w.shape[1]
    spots = cotangent.shape[2]
    count = lax.axis_size("chan")
    ring = lax.axis_size("frames")
    scale = 1.0 / math.sqrt(frames * ring * height * cols)
    taps = spatial_w.shape[0] * spatial_w.shape[1]

    pieces = [cotangent[0]]
    pieces += [swap(pieces[0], "chan", k) for k in range(1, count)]
    across = [(i, (i + (1 if i % 2 else -1)) % ring) for i in range(ring)]
    sums, pooled, weights = prep(inputs, saved, spatial_w)
    groups = [[k] for k in range(count)]
    order = {k: (i, j if len(g) > 1 else None) for i, g in enumerate(groups) for j, k in enumerate(g)}
    outer = []
    for group in groups:
        value = pieces[group[0]] if len(group) == 1 else jnp.stack([pieces[k] for k in group])
        if group == [1]:
            outer.append(swap(outer[0], "chan", 1))
        else:
            outer.append(lax.ppermute(value, "frames", across))

    near = [pieces[0], jnp.stack(pieces[1:])]
    inner = [swap(value, "frames", 1) for value in near]
    near_order = {k: (0, None) if k == 0 else (1, k - 1) for k in range(count)}

    slices = taps + 3
    limit = pltpu.CompilerParams(vmem_limit_bytes=20 << 20)
    part_shape = shape((slices, quarter, channels), F32)
    half_shapes = [shape((n, quarter, channels), F32) for n in (taps - slices // 2, slices - taps)]
    base, g_near, part = pl.pallas_call(
        functools.partial(near_kernel, scale, count, near_order, len(inner)),
        out_shape=(shape((channels, spots), F32), shape((channels, spots), BF16), part_shape),
        in_specs=vmem(count + len(inner) + 3),
        out_specs=tuple(vmem(3)),
        scratch_shapes=[pltpu.VMEM((2, count, quarter, spots), BF16)],
        compiler_params=limit,
        cost_estimate=cost(1 << 30, 4 << 20),
        name="near",
    )(*pieces, *inner, sums, pooled, temporal_w)
    g_far, send_a, send_b, cells = pl.pallas_call(
        functools.partial(far_kernel, scale, count, order, len(outer)),
        out_shape=(
            shape((channels, spots), BF16),
            *half_shapes,
            shape((count, quarter, spots), BF16),
        ),
        in_specs=vmem(len(outer) + 5),
        out_specs=tuple(vmem(4)),
        compiler_params=limit,
        cost_estimate=cost(1 << 29, 4 << 20),
        name="far",
    )(*outer, base, part, sums, pooled, temporal_w)
    keep = pl.pallas_call(
        functools.partial(keep_kernel, scale),
        out_shape=tuple(half_shapes),
        in_specs=vmem(5),
        out_specs=tuple(vmem(2)),
        compiler_params=limit,
        cost_estimate=cost(1 << 28, 4 << 20),
        name="keep",
    )(part, sums, pooled, g_far, cells)

    hbm = pl.BlockSpec(memory_space=pltpu.HBM)
    back = dict(
        scratch_shapes=[
            pltpu.VMEM((height // 2, 4 * quarter, cols), F32),
            pltpu.VMEM((quarter * height, cols), F32),
            pltpu.VMEM((quarter, height, cols), BF16),
            pltpu.SemaphoreType.DMA,
        ],
        compiler_params=limit,
        cost_estimate=cost(3 << 29, 2 << 20),
    )
    input_grad, combined = pl.pallas_call(
        back_near_kernel,
        out_shape=(shape(inputs.shape, BF16), shape((3, 4 * quarter, channels), BF16)),
        in_specs=vmem(2),
        out_specs=(hbm, *vmem(1)),
        name="back_near",
        **back,
    )(g_near, weights)
    input_grad = pl.pallas_call(
        back_far_kernel,
        out_shape=shape(inputs.shape, BF16),
        in_specs=[*vmem(2), hbm],
        out_specs=hbm,
        input_output_aliases={2: 0},
        name="back_far",
        **back,
    )(g_far, combined, input_grad)

    mine, other = reduce_frames(keep, (send_a, send_b))
    sums_out = dict(
        out_shape=(
            shape((taps, quarter, channels), F32),
            shape((slices - taps, quarter, channels), F32),
        ),
        out_specs=(pl.BlockSpec(memory_space=pltpu.HBM),) * 2,
        scratch_shapes=[pltpu.SemaphoreType.DMA((3,))],
        compiler_params=limit,
        cost_estimate=cost(0, 4 << 20),
    )
    begun = pl.pallas_call(early_kernel, in_specs=vmem(3), name="early", **sums_out)(*mine, other[0])
    spatial, temporal = pl.pallas_call(
        finish_kernel,
        in_specs=vmem(1) + [pl.BlockSpec(memory_space=pltpu.HBM)] * 2,
        input_output_aliases={1: 0, 2: 1},
        name="finish",
        **sums_out,
    )(other[1], *begun)
    return (input_grad, spatial.reshape(spatial_w.shape), temporal)


def solution(mesh):
    return jax.shard_map(
        shards,
        mesh=mesh,
        in_specs=(
            P("frames", "chan", None, None),
            P("frames", "chan", None, None),
            P("frames", "chan", None),
            P(None, None, "chan", None),
            P(),
        ),
        out_specs=(
            P("frames", "chan", None, None),
            P(None, None, "chan", None),
            P(None, "chan", None),
        ),
        check_vma=False,
    )
```
